512 devices in a mesh: sample: 32 (over z_hi, y, core), space: 16 (over z_lo, x).
Axes of the slice: x: 4, y: 8, z: 8 (z_hi: 2, z_lo: 4; z = z_hi * 4 + z_lo), core: 2. Of those that a mesh axis runs over, the one named last changes fastest.
Arguments:
- volumes: bfloat16 [512, 32, 8192], P('sample', None, 'space'), may hold values from -6 to 6
- grad_out: bfloat16 [512, 128, 1024], P(('sample', 'space')), may hold values from -6 to 6
- kernel_first: bfloat16 [27, 64, 32], replicated, may hold values from -0.21875 to 0.21875
- bias_first: float32 [64], replicated, may hold values from -3 to 3
- kernel_second: bfloat16 [27, 128, 64], replicated, may hold values from -0.15625 to 0.15625
- bias_second: float32 [128], replicated, may hold values from -3 to 3
Outputs:
- features: bfloat16 [512, 128, 1024], P(('sample', 'space'))
- kernel_grad_first: float32 [27, 64, 32], replicated
- bias_grad_first: float32 [64], replicated
- kernel_grad_second: float32 [27, 128, 64], replicated
- bias_grad_second: float32 [128], replicated
The draws below stay inside these ranges and needn't reach their ends.
All inputs are finite; a program needn't handle non-finite values.
Results may differ from the reference program's by a relative error of at most 0.0085.
The reference program's roundings to bfloat16 on the way (of `pooled`, `delta_two`, `spread` and `delta_one`) count: a program that leaves them out, or rounds other values in their place, can miss the bound.
Values may be sent and summed in bfloat16 or wider, within the bound.
A program may use at most 192 MiB of HBM per device.

```python
import math
import jax
import jax.numpy as jnp
from jax import lax

C0 = 32
C1 = 64
C2 = 128
SIDE = 8
BATCH = 512
DEPTH = 128
DEPTH2 = 64
SIDE2 = 4


def levels(own_key, shape, split, low, high):
    def one(axis_at, parts):
        heights = jax.random.uniform(jax.random.fold_in(jax.random.fold_in(own_key, 6), axis_at), (parts,), jnp.float32, low / len(split), high / len(split))
        return jnp.repeat(jnp.exp(heights), shape[axis_at] // parts).reshape((-1,) + (1,) * (len(shape) - axis_at - 1))

    loudness = one(*split[0])
    for cut in split[1:]:
        loudness = loudness * one(*cut)
    return loudness


def scatter_about(rng, dims, width, reach, split=(), kind=jnp.bfloat16):
    values = jax.random.normal(rng, dims, jnp.float32) * width
    if len(split) > 0:
        values = levels(rng, dims, split, -0.22, 0.18) * values
    return jnp.clip(values, min=-reach, max=reach).astype(kind)


def setup_inputs(seed: int = 0) -> dict:
    seeds = jax.random.split(jax.random.key(seed), 7)
    volumes = scatter_about(seeds[0], (BATCH, C0, DEPTH * SIDE * SIDE), 1.0, 6.0, ((0, 32), (2, 16)))
    grad_out = scatter_about(seeds[1], (BATCH, C2, DEPTH2 * SIDE2 * SIDE2), 1.0, 6.0, ((0, 512),))
    kernel_first = scatter_about(seeds[2], (27, C1, C0), (27 * C0) ** -0.5, 0.21875)
    bias_first = scatter_about(seeds[3], (C1,), 0.5, 3.0, (), jnp.float32)
    kernel_second = scatter_about(seeds[4], (27, C2, C1), (27 * C1) ** -0.5, 0.15625)
    bias_second = scatter_about(seeds[5], (C2,), 0.5, 3.0, (), jnp.float32)
    return dict(volumes=volumes, grad_out=grad_out, kernel_first=kernel_first, bias_first=bias_first, kernel_second=kernel_second, bias_second=bias_second)


LEAK_SLOPE = 0.3

def leaky_unit(values):
    return jnp.where(values > 0, values, LEAK_SLOPE * values)

def leaky_slope(values):
    return jnp.where(values > 0, 1.0, LEAK_SLOPE).astype(values.dtype)

def pad_cube(flat, depth_len, side_len):
    cube_view = flat.reshape(flat.shape[0], flat.shape[1], depth_len, side_len, side_len)
    return jnp.pad(cube_view, ((0, 0), (0, 0), (1, 1), (1, 1), (1, 1)))

def tap_window(padded, tap_index, depth_len, side_len, mirror):
    deep_off = tap_index // 9
    high_off = tap_index // 3 % 3
    wide_off = tap_index % 3
    if mirror:
        deep_off, high_off, wide_off = (2 - deep_off, 2 - high_off, 2 - wide_off)
    window = padded[:, :, deep_off:deep_off + depth_len, high_off:high_off + side_len, wide_off:wide_off + side_len]
    return window.reshape(padded.shape[0], padded.shape[1], depth_len * side_len * side_len)

def convolve(padded, weight, depth_len, side_len):
    summed = jnp.zeros((padded.shape[0], weight.shape[1], depth_len * side_len * side_len), jnp.float32)
    for tap_index in range(27):
        window = tap_window(padded, tap_index, depth_len, side_len, False).astype(jnp.float32)
        summed = summed + jnp.einsum('oc,vcn->von', weight[tap_index].astype(jnp.float32), window)
    return summed

def weight_grad(gradient, padded, depth_len, side_len):
    rows = []
    for tap_index in range(27):
        window = tap_window(padded, tap_index, depth_len, side_len, False).astype(jnp.float32)
        rows.append(jnp.einsum('von,vcn->oc', gradient.astype(jnp.float32), window))
    return jnp.stack(rows)

def spread_back(delta, weight, depth_len, side_len):
    padded = pad_cube(delta, depth_len, side_len)
    summed = jnp.zeros((delta.shape[0], weight.shape[2], depth_len * side_len * side_len), jnp.float32)
    for tap_index in range(27):
        window = tap_window(padded, tap_index, depth_len, side_len, True).astype(jnp.float32)
        summed = summed + jnp.einsum('oc,von->vcn', weight[tap_index].astype(jnp.float32), window)
    return summed

def pool_mean(values, depth_len, side_len):
    lead_dim, chan_dim = (values.shape[0], values.shape[1])
    cube_view = values.reshape(lead_dim, chan_dim, depth_len // 2, 2, side_len // 2, 2, side_len // 2, 2)
    return lax.optimization_barrier(jnp.mean(cube_view, axis=(3, 5, 7))).reshape(lead_dim, chan_dim, -1)

def unpool_even(values, depth_len, side_len):
    lead_dim, chan_dim = (values.shape[0], values.shape[1])
    shape_small = (lead_dim, chan_dim, depth_len // 2, 1, side_len // 2, 1, side_len // 2, 1)
    shape_large = (lead_dim, chan_dim, depth_len // 2, 2, side_len // 2, 2, side_len // 2, 2)
    cube_view = jnp.broadcast_to(values.reshape(shape_small), shape_large)
    return cube_view.reshape(lead_dim, chan_dim, -1)

def reference(volumes, grad_out, kernel_first, bias_first, kernel_second, bias_second):

    def one_volume(running, scan_item):
        kernel_one, bias_one, kernel_two, bias_two = running
        volume, cotangent = scan_item
        volume = volume[None]
        cotangent = cotangent[None]
        padded_in = pad_cube(volume, DEPTH, SIDE)
        first_pre = convolve(padded_in, kernel_first, DEPTH, SIDE) + bias_first[None, :, None]
        pooled = pool_mean(leaky_unit(first_pre), DEPTH, SIDE).astype(jnp.bfloat16)
        padded_mid = pad_cube(pooled, DEPTH2, SIDE2)
        second = convolve(padded_mid, kernel_second, DEPTH2, SIDE2) + bias_second[None, :, None]
        features = leaky_unit(second).astype(jnp.bfloat16)
        delta_two = (cotangent.astype(jnp.float32) * leaky_slope(second)).astype(jnp.bfloat16)
        kernel_two = kernel_two + weight_grad(delta_two, padded_mid, DEPTH2, SIDE2)
        bias_two = bias_two + lax.optimization_barrier(jnp.sum(delta_two.astype(jnp.float32), axis=(0, 2)))
        spread = spread_back(delta_two, kernel_second, DEPTH2, SIDE2).astype(jnp.bfloat16)
        delta_one = (unpool_even(spread.astype(jnp.float32), DEPTH, SIDE) * 0.125 * leaky_slope(first_pre)).astype(jnp.bfloat16)
        kernel_one = kernel_one + weight_grad(delta_one, padded_in, DEPTH, SIDE)
        bias_one = bias_one + lax.optimization_barrier(jnp.sum(delta_one.astype(jnp.float32), axis=(0, 2)))
        return ((kernel_one, bias_one, kernel_two, bias_two), features[0])
    start = (jnp.zeros((27, C1, C0), jnp.float32), jnp.zeros((C1,), jnp.float32), jnp.zeros((27, C2, C1), jnp.float32), jnp.zeros((C2,), jnp.float32))
    running, features = lax.scan(one_volume, start, (volumes, grad_out))
    scale_one = 1.0 / math.sqrt(BATCH * DEPTH * SIDE * SIDE)
    scale_two = 1.0 / math.sqrt(BATCH * DEPTH2 * SIDE2 * SIDE2)
    return (features, running[0] * scale_one, running[1] * scale_one, running[2] * scale_two, running[3] * scale_two)
```

```python
import functools
import math

import jax
import jax.numpy as jnp
from jax import lax
from jax.experimental import pallas as pl
from jax.experimental.pallas import tpu as pltpu
from jax.sharding import PartitionSpec as P

LEAK_SLOPE = 0.3
BF = jnp.bfloat16
F32 = jnp.float32
MESH = pl.DeviceIdType.MESH
LANES = 128
PARTS = 8
TILES = 17
SLOTS = 24


def lane_iota(rows):
    return lax.broadcasted_iota(jnp.int32, (rows, LANES), 1)


def dot(a, b, ca=1, cb=0):
    return lax.dot_general(a, b, (((ca,), (cb,)), ((), ())), preferred_element_type=F32)


def column(row, n):
    r = lax.broadcasted_iota(jnp.int32, (n, n), 0)
    c = lax.broadcasted_iota(jnp.int32, (n, n), 1)
    return jnp.sum(jnp.where(r == c, jnp.broadcast_to(row, (n, n)), 0.0), axis=1, keepdims=True)


def tap_masks(rows, side, mirror):
    lane = lane_iota(rows)
    h = (lane // side) % side
    w = lane % side
    out = []
    for t in range(9):
        dh, dw = t // 3 - 1, t % 3 - 1
        if mirror:
            dh, dw = -dh, -dw
        ok = (h + dh >= 0) & (h + dh < side) & (w + dw >= 0) & (w + dw < side)
        mask = jnp.where(ok, 1.0, 0.0).astype(BF) if (dh or dw) else None
        out.append((mask, (-(dh * side + dw)) % LANES))
    return out


def taps_of(x, masks):
    return [x if m is None else pltpu.roll(x, s, 1) * m for m, s in masks]


def pool_matrix(value, transpose):
    shape = (LANES, 4 * LANES) if transpose else (4 * LANES, LANES)
    big = lax.broadcasted_iota(jnp.int32, shape, 1 if transpose else 0)
    small = lax.broadcasted_iota(jnp.int32, shape, 0 if transpose else 1)
    q, lane = big // LANES, big % LANES
    target = (lane // 64) * 64 + q * 16 + ((lane % 64) // 16) * 4 + (lane % 8) // 2
    return jnp.where(target == small, value, 0.0).astype(BF)


def split_pair(pair, lo):
    top, bottom = pair[:32], pair[32:]
    return (
        jnp.where(lo, top, pltpu.roll(bottom, 64, 1)),
        jnp.where(lo, pltpu.roll(top, 64, 1), bottom),
    )


def join_pair(first, second, lo):
    return (
        jnp.where(lo, first, pltpu.roll(second, 64, 1)),
        jnp.where(lo, pltpu.roll(first, 64, 1), second),
    )


def first_forward(vol, before, after, k1, b1, send, s9, keep, w1, yb):
    lo = lane_iota(32) < 64
    masks = tap_masks(32, 8, False)

    def put(x, s, j):
        for t, y in enumerate(taps_of(x, masks)):
            s9[s, 32 * t : 32 * t + 32, LANES * j : LANES * j + LANES] = y

    @pl.loop(0, 4)
    def _(t):
        at = pl.ds(pl.multiple_of(t * LANES, LANES), LANES)
        for j in range(8):
            a, b = vol[2 * j, :, at], vol[2 * j + 1, :, at]
            put(jnp.where(lo, a, pltpu.roll(b, 64, 1)), 2 * t + 1, j)
            put(jnp.where(lo, pltpu.roll(a, 64, 1), b), 2 * t + 2, j)

    for t in range(27):
        w1[:, 32 * t : 32 * t + 32] = k1[t]

    for j in range(8):
        a, b = before[2 * j], before[2 * j + 1]
        put(jnp.where(lo, pltpu.roll(a, 64, 1), b), 0, j)
        a, b = after[2 * j], after[2 * j + 1]
        put(jnp.where(lo, a, pltpu.roll(b, 64, 1)), 9, j)

    bias = column(b1[...], 64)

    @pl.loop(0, 4)
    def _(q):
        total = None
        for r in range(2):
            pre = dot(w1[...], s9[pl.ds(2 * q + r, 3)].reshape(864, 1024)) + bias
            positive = pre > 0
            keep[2 * q + r] = jnp.where(positive, 1.0, 0.0).astype(BF)
            act = jnp.where(positive, pre, LEAK_SLOPE * pre)
            total = act if total is None else total + act
        high = total.astype(BF)
        low = (total - high.astype(F32)).astype(BF)
        at = pl.ds(pl.multiple_of(q * LANES, LANES), LANES)
        for j in range(8):
            cut = slice(LANES * j, LANES * j + LANES)
            yb[LANES * j : LANES * j + 64, at] = high[:, cut]
            yb[LANES * j + 64 : LANES * j + LANES, at] = low[:, cut]

    z = dot(yb[...], pool_matrix(0.125, False))
    for j in range(8):
        pooled = z[LANES * j : LANES * j + 64] + z[LANES * j + 64 : LANES * j + LANES]
        one, two = split_pair(pooled, lo)
        send[2 * j] = one.astype(BF)
        send[2 * j + 1] = two.astype(BF)


def shift_planes(x, by):
    lane = lax.broadcasted_iota(jnp.int32, x.shape, 1)
    zero = jnp.zeros_like(x)
    if by > 0:
        return jnp.where(lane < 16, zero, pltpu.roll(x, 16, 1))
    return jnp.where(lane >= 1008, zero, pltpu.roll(x, 1008, 1))


def second_layer(recv, k2, b2, grad, features, send, acc2, bias_out, w2, wb, s9b, d9):
    lo = lane_iota(32) < 64
    forward = tap_masks(64, 4, False)
    for i in range(8):
        cut = slice(LANES * i, LANES * i + LANES)
        top, bottom = join_pair(recv[2 * i], recv[2 * i + 1], lo)
        x = jnp.concatenate([top, bottom], axis=0)
        for t, y in enumerate(taps_of(x, forward)):
            s9b[64 * t : 64 * t + 64, cut] = y

    for t in range(27):
        a, n = t // 9, t % 9
        w2[128 * a : 128 * a + 128, 64 * n : 64 * n + 64] = k2[t]
        wb[128 * n : 128 * n + 128, 64 * a : 64 * a + 64] = k2[t]

    p3 = dot(w2[...], s9b[...])
    second = shift_planes(p3[0:128], 1) + p3[128:256] + shift_planes(p3[256:384], -1)
    second = second + column(b2[...], 128)
    positive = second > 0
    features[0] = jnp.where(positive, second, LEAK_SLOPE * second).astype(BF)
    delta = (grad[0].astype(F32) * jnp.where(positive, 1.0, LEAK_SLOPE)).astype(BF)

    backward = tap_masks(128, 4, True)
    for i in range(8):
        cut = slice(LANES * i, LANES * i + LANES)
        for t, y in enumerate(taps_of(delta[:, cut], backward)):
            d9[128 * t : 128 * t + 128, cut] = y
    r3 = dot(wb[...], d9[...], 0, 0)
    spread = shift_planes(r3[0:64], -1) + r3[64:128] + shift_planes(r3[128:192], 1)
    for i in range(8):
        one, two = split_pair(spread[:, LANES * i : LANES * i + LANES], lo)
        send[2 * i] = one.astype(BF)
        send[2 * i + 1] = two.astype(BF)

    d3 = (shift_planes(delta, -1), delta, shift_planes(delta, 1))
    for a in range(3):
        acc2[128 * a : 128 * a + 128, 0:576] = dot(d3[a], s9b[...], 1, 1)
    bias_out[...] = dot(jnp.ones((8, 1024), BF), delta, 1, 1)


def first_backward(recv, s9, keep, acc1, bias_out, tt, dr):
    lo = lane_iota(32) < 64
    for j in range(8):
        top, bottom = join_pair(recv[2 * j], recv[2 * j + 1], lo)
        tt[64 * j : 64 * j + 32] = top
        tt[64 * j + 32 : 64 * j + 64] = bottom
    for i in (0, 1, 10, 11):
        dr[i] = jnp.zeros((64, 1024), BF)
    spread_to = pool_matrix(1.0, True)
    for q in range(4):
        u = dot(tt[...], spread_to[:, LANES * q : LANES * q + LANES])
        for r in range(2):
            p = 2 * q + r
            for j in range(8):
                cut = slice(LANES * j, LANES * j + LANES)
                slope = jnp.where(keep[p, :, cut] > 0, 1.0, LEAK_SLOPE).astype(F32)
                dr[9 - p, :, cut] = (u[64 * j : 64 * j + 64] * 0.125 * slope).astype(BF)

    acc1[:, 0:288] = jnp.zeros((192, 288), F32)
    bias_out[...] = jnp.zeros((8, 64), F32)

    @pl.loop(0, 10)
    def _(s):
        acc1[:, 0:288] += dot(dr[pl.ds(9 - s, 3)].reshape(192, 1024), s9[s], 1, 1)

    @pl.loop(2, 10)
    def _(i):
        bias_out[...] += dot(jnp.ones((8, 1024), BF), dr[i], 1, 1)


def position():
    sample, space = lax.axis_index("sample"), lax.axis_index("space")
    core = sample % 2
    y = (sample // 2) % 8
    z = (sample // 16) * 4 + space // 4
    x = space % 4
    return core, x, y, z


def device(core, x, y, z):
    return ((z // 4) * 16 + y * 2 + core, (z % 4) * 4 + x)


def greet(peers):
    barrier = pltpu.get_barrier_semaphore()
    for peer in peers:
        pl.semaphore_signal(barrier, inc=1, device_id=peer, device_id_type=MESH)
    pl.semaphore_wait(barrier, len(peers))


def space_peers():
    sample, space = lax.axis_index("sample"), lax.axis_index("space")
    return [(sample, (space + k) % 16) for k in range(1, 16)]


def exchange(send, recv, ssem, rsem):
    me = lax.axis_index("space")
    copies = []
    for k, peer in enumerate(space_peers()):
        copy = pltpu.make_async_remote_copy(
            src_ref=send.at[peer[1]], dst_ref=recv.at[me], send_sem=ssem.at[k],
            recv_sem=rsem.at[k], device_id=peer, device_id_type=MESH,
        )
        copy.start()
        copies.append(copy)
    recv[me] = send[me]
    return copies


def grad_peers():
    core, x, y, z = position()
    out = [device(1 - core, x, y, z)]
    out += [device(core, (x + k) % 4, y, z) for k in range(1, 4)]
    out += [device(core, x, (y + k) % 8, z) for k in range(1, 8)]
    out += [device(core, x, y, (z + k) % 8) for k in range(1, 8)]
    return out


def pack_tiles(acc1, bias1, acc2, bias2, g):
    lane = lane_iota(16)
    row = lax.broadcasted_iota(jnp.int32, (16, LANES), 0)
    lo = lane < 64

    def put(t, value):
        g[t // TILES, t % TILES] = value.astype(BF)

    for r in range(24):
        for c in range(4):
            put(4 * r + c, acc2[16 * r : 16 * r + 16, LANES * c : LANES * c + LANES])
    for k in range(12):
        left = acc2[16 * k : 16 * k + 16, 512:640]
        right = acc2[192 + 16 * k : 208 + 16 * k, 512:640]
        put(96 + k, jnp.where(lo, left, pltpu.roll(right, 64, 1)))
    for r in range(12):
        for c in range(2):
            put(108 + 2 * r + c, acc1[16 * r : 16 * r + 16, LANES * c : LANES * c + LANES])
    for k in range(3):
        tile = acc1[16 * k : 16 * k + 16, 256:384]
        for n in range(1, 4):
            at = 48 * n + 16 * k
            tile = jnp.where(lane >= 32 * n, pltpu.roll(acc1[at : at + 16, 256:384], 32 * n, 1), tile)
        put(132 + k, tile)
    one = jnp.concatenate([bias1[0:1], jnp.zeros((1, 64), F32)], axis=1)
    one = jnp.broadcast_to(one, (16, LANES))
    two = jnp.broadcast_to(bias2[0:1], (16, LANES))
    put(135, jnp.where(row == 0, one, jnp.where(row == 1, two, 0.0)))


def unpack_tiles(c, out1, outb1, out2, outb2, scale_one, scale_two):
    def get(t, scale):
        return c[t // TILES, t % TILES].astype(F32) * scale

    def put2(r, n, value):
        out2[9 * (r // 8) + n, 16 * (r % 8) : 16 * (r % 8) + 16] = value

    def put1(r, n, value):
        out1[9 * (r // 4) + n, 16 * (r % 4) : 16 * (r % 4) + 16] = value

    for r in range(24):
        for n in range(4):
            v = get(4 * r + n, scale_two)
            put2(r, 2 * n, v[:, 0:64])
            put2(r, 2 * n + 1, v[:, 64:128])
    for k in range(12):
        v = get(96 + k, scale_two)
        put2(k, 8, v[:, 0:64])
        put2(12 + k, 8, v[:, 64:128])
    for r in range(12):
        for n in range(2):
            v = get(108 + 2 * r + n, scale_one)
            for i in range(4):
                put1(r, 4 * n + i, v[:, 32 * i : 32 * i + 32])
    for k in range(3):
        v = get(132 + k, scale_one)
        for n in range(4):
            put1(3 * n + k, 8, v[:, 32 * n : 32 * n + 32])
    v = c[135 // TILES, 135 % TILES].astype(F32)
    outb1[...] = v[0:1, 0:64] * scale_one
    outb2[...] = v[1:2] * scale_two


def reduce_all(g, rc, xs, rx, ys, ry, rz, fs, ay, bx, call, ssem, rsem):
    core, x, y, z = position()
    started = []

    def send(i, src, dst, peer):
        copy = pltpu.make_async_remote_copy(
            src_ref=src, dst_ref=dst, send_sem=ssem.at[i], recv_sem=rsem.at[i],
            device_id=peer, device_id_type=MESH,
        )
        copy.start()
        started.append(copy)
        return copy

    other = device(1 - core, x, y, z)
    xp = [device(core, (x + k) % 4, y, z) for k in range(1, 4)]
    yp = [device(core, x, (y + k) % 8, z) for k in range(1, 8)]
    zp = [device(core, x, y, (z + k) % 8) for k in range(1, 8)]

    send(0, g.at[pl.ds((1 - core) * 4, 4)], rc, other).wait_recv()

    @pl.loop(0, 4)
    def _(n):
        xs[n] = (g[core * 4 + n].astype(F32) + rc[n].astype(F32)).astype(BF)

    now = [send(1 + k, xs.at[(x + k + 1) % 4], rx.at[k], xp[k]) for k in range(3)]
    for copy in now:
        copy.wait_recv()
    total = xs[x].astype(F32)
    for k in range(3):
        total = total + rx[k].astype(F32)
    ys[0:TILES] = total.astype(BF)
    ys[TILES:SLOTS] = jnp.zeros((SLOTS - TILES, 16, LANES), BF)

    now = [send(4 + k, ys.at[pl.ds(((y + k + 1) % 8) * 3, 3)], ry.at[k], yp[k]) for k in range(7)]
    for copy in now:
        copy.wait_recv()
    total = ys[pl.ds(y * 3, 3)].astype(F32)
    for k in range(7):
        total = total + ry[k].astype(F32)
    fs[...] = total.astype(BF)
    rz[z] = total.astype(BF)

    now = [send(11 + k, fs, rz.at[z], zp[k]) for k in range(7)]
    for copy in now:
        copy.wait_recv()
    total = rz[0].astype(F32)
    for k in range(1, 8):
        total = total + rz[k].astype(F32)
    ay[pl.ds(y * 3, 3)] = total.astype(BF)

    now = [send(18 + k, ay.at[pl.ds(y * 3, 3)], ay.at[pl.ds(y * 3, 3)], yp[k]) for k in range(7)]
    for copy in now:
        copy.wait_recv()
    bx[x] = ay[0:TILES]

    now = [send(25 + k, ay.at[0:TILES], bx.at[x], xp[k]) for k in range(3)]
    for copy in now:
        copy.wait_recv()

    now = send(28, bx, call.at[pl.ds(core * 4, 4)], other)

    @pl.loop(0, 4)
    def _(n):
        call[core * 4 + n] = bx[n]

    now.wait_recv()
    for copy in started:
        copy.wait_send()


REDUCE_SCRATCH = [
    pltpu.VMEM((PARTS, TILES, 16, LANES), BF),
    pltpu.VMEM((4, TILES, 16, LANES), BF),
    pltpu.VMEM((4, TILES, 16, LANES), BF),
    pltpu.VMEM((3, TILES, 16, LANES), BF),
    pltpu.VMEM((SLOTS, 16, LANES), BF),
    pltpu.VMEM((7, 3, 16, LANES), BF),
    pltpu.VMEM((8, 3, 16, LANES), BF),
    pltpu.VMEM((3, 16, LANES), BF),
    pltpu.VMEM((SLOTS, 16, LANES), BF),
    pltpu.VMEM((4, TILES, 16, LANES), BF),
    pltpu.VMEM((PARTS, TILES, 16, LANES), BF),
    pltpu.SemaphoreType.DMA((29,)),
    pltpu.SemaphoreType.DMA((29,)),
]


def shape(dims, kind=BF):
    return jax.ShapeDtypeStruct(dims, kind)


def call_kernel(body, outs, scratch, operands, name, cid=None):
    vmem = pl.BlockSpec(memory_space=pltpu.VMEM)
    return pl.pallas_call(
        body,
        name=name,
        out_shape=outs,
        in_specs=[vmem] * len(operands),
        out_specs=[vmem] * len(outs),
        scratch_shapes=scratch,
        compiler_params=pltpu.CompilerParams(
            vmem_limit_bytes=48 << 20,
            collective_id=cid,
            has_side_effects=cid is not None,
        ),
    )(*operands)


def exchange_kernel(send, recv, ssem, rsem):
    greet(space_peers())
    for copy in exchange(send, recv, ssem, rsem):
        copy.wait()


def swap(send, cid):
    return call_kernel(
        exchange_kernel, [shape((16, 32, LANES))],
        [pltpu.SemaphoreType.DMA((15,)), pltpu.SemaphoreType.DMA((15,))], [send], "swap", cid,
    )[0]


def reduce_kernel(scale_one, scale_two, acc1, bias1, acc2, bias2, out1, outb1, out2, outb2, g, *rest):
    pack_tiles(acc1, bias1, acc2, bias2, g)
    greet(grad_peers())
    reduce_all(g, *rest)
    unpack_tiles(rest[9], out1, outb1, out2, outb2, scale_one, scale_two)


def on_device(volumes, grad_out, kernel_first, bias_first, kernel_second, bias_second):
    devices = lax.axis_size("sample") * lax.axis_size("space")
    size = lax.axis_size("space")
    scale_one = 1.0 / math.sqrt(volumes.shape[0] * volumes.shape[2] * devices)
    scale_two = 1.0 / math.sqrt(grad_out.shape[0] * grad_out.shape[2] * devices)
    up = [(i, i + 1) for i in range(size - 1)]
    down = [(j, i) for i, j in up]
    before = lax.ppermute(volumes[:, :, 384:512], "space", up)
    after = lax.ppermute(volumes[:, :, 0:128], "space", down)

    send, s9, keep = call_kernel(
        first_forward,
        [shape((16, 32, LANES)), shape((10, 288, 1024)), shape((8, 64, 1024))],
        [pltpu.VMEM((64, 864), BF), pltpu.VMEM((1024, 512), BF)],
        [volumes, before, after, kernel_first, bias_first.reshape(1, -1)],
        "first_forward",
    )
    recv = swap(send, 0)
    features, send, acc2, bias2 = call_kernel(
        second_layer,
        [shape((1, 128, 1024)), shape((16, 32, LANES)), shape((384, 640), F32), shape((8, 128), F32)],
        [
            pltpu.VMEM((384, 576), BF),
            pltpu.VMEM((1152, 192), BF),
            pltpu.VMEM((576, 1024), BF),
            pltpu.VMEM((1152, 1024), BF),
        ],
        [recv, kernel_second, bias_second.reshape(1, -1), grad_out],
        "second_layer",
    )
    recv = swap(send, 1)
    acc1, bias1 = call_kernel(
        first_backward,
        [shape((192, 384), F32), shape((8, 64), F32)],
        [pltpu.VMEM((512, LANES), BF), pltpu.VMEM((12, 64, 1024), BF)],
        [recv, s9, keep],
        "first_backward",
    )
    out1, outb1, out2, outb2 = call_kernel(
        functools.partial(reduce_kernel, scale_one, scale_two),
        [shape((27, 64, 32), F32), shape((1, 64), F32), shape((27, 128, 64), F32), shape((1, 128), F32)],
        REDUCE_SCRATCH,
        [acc1, bias1, acc2, bias2],
        "reduce",
        2,
    )
    return features, out1, outb1.reshape(-1), out2, outb2.reshape(-1)


def solution(mesh):
    in_specs = (P("sample", None, "space"), P(("sample", "space"), None, None), P(), P(), P(), P())
    out_specs = (P(("sample", "space"), None, None), P(), P(), P(), P())
    return jax.shard_map(
        on_device, mesh=mesh, in_specs=in_specs, out_specs=out_specs, check_vma=False
    )
```

```python
import math

import jax
import jax.numpy as jnp
from jax import lax
from jax.experimental import pallas as pl
from jax.experimental.pallas import tpu as pltpu
from jax.sharding import PartitionSpec as P

LEAK_SLOPE = 0.3
BF = jnp.bfloat16
F32 = jnp.float32
MESH = pl.DeviceIdType.MESH
LANES = 128
PARTS = 8
TILES1, ROWS1 = 7, 8
TILES2, ROWS2 = 14, 16


def lane_iota(rows):
    return lax.broadcasted_iota(jnp.int32, (rows, LANES), 1)


def dot(a, b, ca=1, cb=0):
    return lax.dot_general(a, b, (((ca,), (cb,)), ((), ())), preferred_element_type=F32)


def column(row, n):
    r = lax.broadcasted_iota(jnp.int32, (n, n), 0)
    c = lax.broadcasted_iota(jnp.int32, (n, n), 1)
    return jnp.sum(jnp.where(r == c, jnp.broadcast_to(row, (n, n)), 0.0), axis=1, keepdims=True)


def row_of(col, n):
    r = lax.broadcasted_iota(jnp.int32, (n, n), 0)
    c = lax.broadcasted_iota(jnp.int32, (n, n), 1)
    return jnp.sum(jnp.where(r == c, jnp.broadcast_to(col, (n, n)), 0.0), axis=0, keepdims=True)


def tap_masks(rows, side, mirror):
    lane = lane_iota(rows)
    h = (lane // side) % side
    w = lane % side
    out = []
    for t in range(9):
        dh, dw = t // 3 - 1, t % 3 - 1
        if mirror:
            dh, dw = -dh, -dw
        ok = (h + dh >= 0) & (h + dh < side) & (w + dw >= 0) & (w + dw < side)
        mask = jnp.where(ok, 1.0, 0.0).astype(BF) if (dh or dw) else None
        out.append((mask, (-(dh * side + dw)) % LANES))
    return out


def taps_of(x, masks):
    return [x if m is None else pltpu.roll(x, s, 1) * m for m, s in masks]


def pool_matrix(value, transpose):
    shape = (LANES, 4 * LANES) if transpose else (4 * LANES, LANES)
    big = lax.broadcasted_iota(jnp.int32, shape, 1 if transpose else 0)
    small = lax.broadcasted_iota(jnp.int32, shape, 0 if transpose else 1)
    q, lane = big // LANES, big % LANES
    target = (lane // 64) * 64 + q * 16 + ((lane % 64) // 16) * 4 + (lane % 8) // 2
    return jnp.where(target == small, value, 0.0).astype(BF)


def split_pair(pair, lo):
    top, bottom = pair[:32], pair[32:]
    return (
        jnp.where(lo, top, pltpu.roll(bottom, 64, 1)),
        jnp.where(lo, pltpu.roll(top, 64, 1), bottom),
    )


def join_pair(first, second, lo):
    return (
        jnp.where(lo, first, pltpu.roll(second, 64, 1)),
        jnp.where(lo, pltpu.roll(first, 64, 1), second),
    )


def position():
    sample, space = lax.axis_index("sample"), lax.axis_index("space")
    core = sample % 2
    y = (sample // 2) % 8
    z = (sample // 16) * 4 + space // 4
    x = space % 4
    return core, x, y, z


def device(core, x, y, z):
    return ((z // 4) * 16 + y * 2 + core, (z % 4) * 4 + x)


def space_peers():
    sample, space = lax.axis_index("sample"), lax.axis_index("space")
    return [(sample, (space + k) % 16) for k in range(1, 16)]


def all_peers():
    core, x, y, z = position()
    out = space_peers()
    out += [device(core, x, (y + k) % 8, z) for k in range(1, 8)]
    out += [device(core, x, y, (1 - z // 4) * 4 + k) for k in range(4)]
    out += [device(1 - core, x, y, z)]
    return out


def remote(src, dst, ssem, rsem, peer):
    return pltpu.make_async_remote_copy(
        src_ref=src, dst_ref=dst, send_sem=ssem, recv_sem=rsem,
        device_id=peer, device_id_type=MESH,
    )


def exchange(send, recv, ssem, rsem):
    me = lax.axis_index("space")
    copies = []
    for k, peer in enumerate(space_peers()):
        copy = remote(send.at[peer[1]], recv.at[me], ssem.at[k], rsem.at[k], peer)
        copy.start()
        copies.append(copy)
    recv[me] = send[me]
    return copies


class Sum:
    def __init__(self, tiles, rows, kind, refs):
        self.tiles, self.rows, self.kind = tiles, rows, kind
        self.share = -(-tiles // 8)
        (self.g, self.rc, self.xs, self.rx, self.ys, self.ry, self.rz, self.fs, self.ay, self.bx,
         self.out, self.ssem, self.rsem) = refs
        self.pos = core, x, y, z = position()
        self.other = device(1 - core, x, y, z)
        self.xp = [device(core, (x + k) % 4, y, z) for k in range(1, 4)]
        self.yp = [device(core, x, (y + k) % 8, z) for k in range(1, 8)]
        self.zp = [device(core, x, y, (z + k) % 8) for k in range(1, 8)]
        self.started, self.now = [], []

    @staticmethod
    def scratch(tiles, rows, kind):
        share = -(-tiles // 8)
        dims = [
            (PARTS, tiles), (4, tiles), (4, tiles), (3, tiles), (8 * share,), (7, share),
            (8, share), (share,), (8 * share,), (4, tiles), (PARTS, tiles),
        ]
        out = [pltpu.VMEM(d + (rows, LANES), kind) for d in dims]
        return out + [pltpu.SemaphoreType.DMA((29,)), pltpu.SemaphoreType.DMA((29,))]

    def send(self, i, src, dst, peer):
        copy = remote(src, dst, self.ssem.at[i], self.rsem.at[i], peer)
        copy.start()
        self.started.append(copy)
        self.now.append(copy)

    def arrive(self):
        for copy in self.now:
            copy.wait_recv()
        self.now = []

    def mine(self, ref):
        return ref.at[pl.ds(self.pos[2] * self.share, self.share)]

    def step(self, i):
        core, x, y, z = self.pos
        kind = self.kind
        if i == 0:
            self.send(0, self.g.at[pl.ds((1 - core) * 4, 4)], self.rc, self.other)
            return
        self.arrive()
        if i == 1:
            for n in range(4):
                self.xs[n] = (self.g[core * 4 + n].astype(F32) + self.rc[n].astype(F32)).astype(kind)
            for k in range(3):
                self.send(1 + k, self.xs.at[(x + k + 1) % 4], self.rx.at[k], self.xp[k])
        elif i == 2:
            total = self.xs[x].astype(F32)
            for k in range(3):
                total = total + self.rx[k].astype(F32)
            self.ys[0 : self.tiles] = total.astype(kind)
            for k in range(7):
                at = pl.ds(((y + k + 1) % 8) * self.share, self.share)
                self.send(4 + k, self.ys.at[at], self.ry.at[k], self.yp[k])
        elif i == 3:
            total = self.ys[pl.ds(y * self.share, self.share)].astype(F32)
            for k in range(7):
                total = total + self.ry[k].astype(F32)
            self.fs[...] = total.astype(kind)
            self.rz[z] = total.astype(kind)
            for k in range(7):
                self.send(11 + k, self.fs, self.rz.at[z], self.zp[k])
        elif i == 4:
            total = self.rz[0].astype(F32)
            for k in range(1, 8):
                total = total + self.rz[k].astype(F32)
            self.ay[pl.ds(y * self.share, self.share)] = total.astype(kind)
            for k in range(7):
                self.send(18 + k, self.mine(self.ay), self.mine(self.ay), self.yp[k])
        elif i == 5:
            for k in range(3):
                self.send(25 + k, self.ay.at[0 : self.tiles], self.bx.at[x], self.xp[k])
            self.bx[x] = self.ay[0 : self.tiles]
        elif i == 6:
            self.send(28, self.bx, self.out.at[pl.ds(core * 4, 4)], self.other)
            for n in range(4):
                self.out[core * 4 + n] = self.bx[n]

    def finish(self):
        for copy in self.started:
            copy.wait_send()


def put_taps(x, masks, s9, s, j):
    for t, y in enumerate(taps_of(x, masks)):
        s9[s, 32 * t : 32 * t + 32, LANES * j : LANES * j + LANES] = y


def inner_taps(vol, s9, masks, lo):
    @pl.loop(0, 4)
    def _(t):
        at = pl.ds(pl.multiple_of(t * LANES, LANES), LANES)
        for j in range(8):
            a, b = vol[2 * j, :, at], vol[2 * j + 1, :, at]
            put_taps(jnp.where(lo, a, pltpu.roll(b, 64, 1)), masks, s9, 2 * t + 1, j)
            put_taps(jnp.where(lo, pltpu.roll(a, 64, 1), b), masks, s9, 2 * t + 2, j)


def outer_taps(before, after, s9, masks, lo):
    for j in range(8):
        a, b = before[2 * j], before[2 * j + 1]
        put_taps(jnp.where(lo, pltpu.roll(a, 64, 1), b), masks, s9, 0, j)
        a, b = after[2 * j], after[2 * j + 1]
        put_taps(jnp.where(lo, a, pltpu.roll(b, 64, 1)), masks, s9, 9, j)


def first_outputs(part, b1, keep, yb, send, lo):
    bias = column(b1[...], 64)

    @pl.loop(0, 4)
    def _(q):
        total = None
        for r in range(2):
            p = 2 * q + r
            pre = part[p, 0:64] + part[p + 1, 64:128] + part[p + 2, 128:192] + bias
            positive = pre > 0
            keep[p] = jnp.where(positive, 1.0, 0.0).astype(BF)
            act = jnp.where(positive, pre, LEAK_SLOPE * pre)
            total = act if total is None else total + act
        high = total.astype(BF)
        low = (total - high.astype(F32)).astype(BF)
        at = pl.ds(pl.multiple_of(q * LANES, LANES), LANES)
        for j in range(8):
            cut = slice(LANES * j, LANES * j + LANES)
            yb[LANES * j : LANES * j + 64, at] = high[:, cut]
            yb[LANES * j + 64 : LANES * j + LANES, at] = low[:, cut]

    z = dot(yb[...], pool_matrix(0.125, False))
    for j in range(8):
        pooled = z[LANES * j : LANES * j + 64] + z[LANES * j + 64 : LANES * j + LANES]
        one, two = split_pair(pooled, lo)
        send[2 * j] = one.astype(BF)
        send[2 * j + 1] = two.astype(BF)


def shift_planes(x, by):
    lane = lax.broadcasted_iota(jnp.int32, x.shape, 1)
    zero = jnp.zeros_like(x)
    if by > 0:
        return jnp.where(lane < 16, zero, pltpu.roll(x, 16, 1))
    return jnp.where(lane >= 1008, zero, pltpu.roll(x, 1008, 1))


def second_layer(recv, w2, wb, b2, grad, features, send, d3, s9b, d9, lo):
    forward = tap_masks(64, 4, False)
    for i in range(8):
        cut = slice(LANES * i, LANES * i + LANES)
        top, bottom = join_pair(recv[2 * i], recv[2 * i + 1], lo)
        x = jnp.concatenate([top, bottom], axis=0)
        for t, y in enumerate(taps_of(x, forward)):
            s9b[64 * t : 64 * t + 64, cut] = y
    p3 = dot(w2[...], s9b[...])
    second = shift_planes(p3[0:128], 1) + p3[128:256] + shift_planes(p3[256:384], -1)
    second = second + column(b2[...], 128)
    positive = second > 0
    features[...] = jnp.where(positive, second, LEAK_SLOPE * second).astype(BF)
    delta = (grad[...].astype(F32) * jnp.where(positive, 1.0, LEAK_SLOPE)).astype(BF)
    d3[128:256] = delta

    backward = tap_masks(128, 4, True)
    for i in range(8):
        cut = slice(LANES * i, LANES * i + LANES)
        for t, y in enumerate(taps_of(delta[:, cut], backward)):
            d9[128 * t : 128 * t + 128, cut] = y
    r3 = dot(wb[...], d9[...])
    spread = shift_planes(r3[0:64], -1) + r3[64:128] + shift_planes(r3[128:192], 1)
    for i in range(8):
        one, two = split_pair(spread[:, LANES * i : LANES * i + LANES], lo)
        send[2 * i] = one.astype(BF)
        send[2 * i + 1] = two.astype(BF)


def second_taps(d3, s9b, acc2, g2):
    delta = d3[128:256]
    d3[0:128] = shift_planes(delta, -1)
    d3[256:384] = shift_planes(delta, 1)
    acc2[...] = dot(s9b[...], d3[...], 1, 1)
    for a in range(3):
        for r in range(36):
            t = 36 * a + r
            tile = acc2[16 * r : 16 * r + 16, LANES * a : LANES * a + LANES]
            g2[t // TILES2, t % TILES2] = tile.astype(BF)
    for t in range(108, PARTS * TILES2):
        g2[t // TILES2, t % TILES2] = jnp.zeros((ROWS2, LANES), BF)
    return row_of(jnp.sum(delta.astype(F32), axis=1, keepdims=True), 128)


def first_deltas(recv, keep, tt, dr, lo):
    for j in range(8):
        top, bottom = join_pair(recv[2 * j], recv[2 * j + 1], lo)
        tt[64 * j : 64 * j + 32] = top
        tt[64 * j + 32 : 64 * j + 64] = bottom
    for i in (0, 1, 10, 11):
        dr[i] = jnp.zeros((64, 1024), BF)
    spread_to = pool_matrix(1.0, True)
    total = jnp.zeros((64, LANES), F32)
    for q in range(4):
        u = dot(tt[...], spread_to[:, LANES * q : LANES * q + LANES])
        for r in range(2):
            p = 2 * q + r
            for j in range(8):
                cut = slice(LANES * j, LANES * j + LANES)
                slope = jnp.where(keep[p, :, cut] > 0, 1.0, LEAK_SLOPE).astype(F32)
                delta = (u[64 * j : 64 * j + 64] * 0.125 * slope).astype(BF)
                dr[9 - p, :, cut] = delta
                total = total + delta.astype(F32)
    return row_of(jnp.sum(total, axis=1, keepdims=True), 64)


def first_taps(s9, dr, acc1, first, last):
    acc = None
    for s in range(first, last):
        term = dot(s9[s], dr[9 - s : 12 - s].reshape(192, 1024), 1, 1)
        acc = term if acc is None else acc + term
    if first == 0:
        acc1[:, 0:192] = acc
    else:
        acc1[:, 0:192] += acc


def pack_first(acc1, bias1, bias2, g1):
    lo = lane_iota(8) < 64
    row = lax.broadcasted_iota(jnp.int32, (8, LANES), 0)

    def put(t, value):
        g1[t // TILES1, t % TILES1] = value

    for k in range(36):
        put(k, acc1[8 * k : 8 * k + 8, 0:LANES])
    for k in range(18):
        left = acc1[8 * k : 8 * k + 8, LANES:256]
        right = acc1[144 + 8 * k : 152 + 8 * k, LANES:256]
        put(36 + k, jnp.where(lo, left, pltpu.roll(right, 64, 1)))
    one = jnp.concatenate([bias1, jnp.zeros((1, 64), F32)], axis=1)
    one = jnp.broadcast_to(one, (8, LANES))
    two = jnp.broadcast_to(bias2, (8, LANES))
    put(54, jnp.where(row == 0, one, jnp.where(row == 1, two, 0.0)))
    put(55, jnp.zeros((8, LANES), F32))


def unpack_first(c, out1, outb):
    def get(t):
        return c[t // TILES1, t % TILES1]

    def put(a, r, value):
        out1[9 * a + r // 4, 8 * (r % 4) : 8 * (r % 4) + 8] = value

    for k in range(36):
        put(0, k, get(k)[:, 0:64])
        put(1, k, get(k)[:, 64:128])
    for k in range(18):
        put(2, k, get(36 + k)[:, 0:64])
        put(2, 18 + k, get(36 + k)[:, 64:128])
    outb[...] = get(54)


def step_kernel(
    vol_in, k1_in, b1, k2_in, b2, grad_in, feat_out, out1, out2, outb,
    vol, k1, k2, grad, feat, before, after, s9, part, keep, w1, yb, send1, recv1,
    w2, wb, s9b, d3, d9, acc2, send2, recv2, tt, dr, acc1,
    lsem, hssem, hrsem, s1, r1, s2, r2, *sums,
):
    space = lax.axis_index("space")
    sample = lax.axis_index("sample")
    n = len(sums) // 2
    sum1 = Sum(TILES1, ROWS1, F32, sums[:n])
    sum2 = Sum(TILES2, ROWS2, BF, sums[n:])
    peers = all_peers()
    barrier = pltpu.get_barrier_semaphore()
    for peer in peers:
        pl.semaphore_signal(barrier, inc=1, device_id=peer, device_id_type=MESH)
    loads = [
        pltpu.make_async_copy(src, dst, lsem.at[i])
        for i, (src, dst) in enumerate(((vol_in, vol), (k1_in, k1), (k2_in, k2), (grad_in.at[0], grad)))
    ]
    for load in loads:
        load.start()

    lo = lane_iota(32) < 64
    masks = tap_masks(32, 8, False)
    loads[0].wait()
    inner_taps(vol, s9, masks, lo)
    loads[1].wait()
    for a in range(3):
        w1[64 * a : 64 * a + 64] = jnp.transpose(k1[9 * a : 9 * a + 9].reshape(288, 64))

    pl.semaphore_wait(barrier, len(peers))
    tail = remote(vol.at[:, :, pl.ds(384, 128)], before, hssem.at[0], hrsem.at[0], (sample, (space + 1) % 16))
    head = remote(vol.at[:, :, pl.ds(0, 128)], after, hssem.at[1], hrsem.at[1], (sample, (space + 15) % 16))

    @pl.when(space < 15)
    def _():
        tail.start()

    @pl.when(space > 0)
    def _():
        head.start()

    @pl.when(space == 0)
    def _():
        before[...] = jnp.zeros_like(before)

    @pl.when(space == 15)
    def _():
        after[...] = jnp.zeros_like(after)

    for s in range(1, 9):
        part[s] = dot(w1[...], s9[s])

    @pl.when(space > 0)
    def _():
        tail.wait_recv()
        head.wait_send()

    @pl.when(space < 15)
    def _():
        head.wait_recv()
        tail.wait_send()

    outer_taps(before, after, s9, masks, lo)
    for s in (0, 9):
        part[s] = dot(w1[...], s9[s])
    first_outputs(part, b1, keep, yb, send1, lo)
    there = exchange(send1, recv1, s1, r1)

    loads[2].wait()
    for a in range(3):
        w2[128 * a : 128 * a + 128] = jnp.transpose(k2[9 * a : 9 * a + 9].reshape(576, 128))
        for t in range(9):
            wb[64 * a : 64 * a + 64, 128 * t : 128 * t + 128] = k2[9 * a + t]
    loads[3].wait()
    for copy in there:
        copy.wait_recv()
    second_layer(recv1, w2, wb, b2, grad, feat, send2, d3, s9b, d9, lo)
    back = exchange(send2, recv2, s2, r2)
    write = pltpu.make_async_copy(feat, feat_out.at[0], lsem.at[4])
    write.start()

    bias2 = second_taps(d3, s9b, acc2, sum2.g)
    for total in (sum1, sum2):
        pad = 8 * total.share - total.tiles
        total.ys[total.tiles : 8 * total.share] = jnp.zeros((pad, total.rows, LANES), total.kind)
    sum2.step(0)
    for copy in back:
        copy.wait_recv()
    sum2.step(1)
    bias1 = first_deltas(recv2, keep, tt, dr, lo)
    first_taps(s9, dr, acc1, 0, 3)
    sum2.step(2)
    first_taps(s9, dr, acc1, 3, 10)
    pack_first(acc1, bias1, bias2, sum1.g)
    sum1.step(0)
    sum2.step(3)
    sum1.step(1)
    sum1.step(2)
    sum2.step(4)
    sum1.step(3)
    sum2.step(5)
    sum1.step(4)
    sum2.step(6)
    sum1.step(5)
    sum2.step(7)
    out2[...] = sum2.out[...]
    sum1.step(6)
    sum1.step(7)
    unpack_first(sum1.out, out1, outb)
    for copy in there + back:
        copy.wait_send()
    sum1.finish()
    sum2.finish()
    write.wait()


def shape(dims, kind=BF):
    return jax.ShapeDtypeStruct(dims, kind)


def on_device(volumes, grad_out, kernel_first, bias_first, kernel_second, bias_second):
    devices = lax.axis_size("sample") * lax.axis_size("space")
    scale_one = 1.0 / math.sqrt(volumes.shape[0] * volumes.shape[2] * devices)
    scale_two = 1.0 / math.sqrt(grad_out.shape[0] * grad_out.shape[2] * devices)
    vmem = pl.BlockSpec(memory_space=pltpu.VMEM)
    anywhere = pl.BlockSpec(memory_space=pl.ANY)
    dma = pltpu.SemaphoreType.DMA
    feat, out1, out2, outb = pl.pallas_call(
        step_kernel,
        name="step",
        out_shape=[
            shape((1, 128, 1024)), shape((27, 32, 64), F32),
            shape((PARTS, TILES2, ROWS2, LANES)), shape((8, LANES), F32),
        ],
        in_specs=[anywhere, anywhere, vmem, anywhere, vmem, anywhere],
        out_specs=[anywhere, vmem, vmem, vmem],
        scratch_shapes=[
            pltpu.VMEM((16, 32, 512), BF),
            pltpu.VMEM((27, 32, 64), BF),
            pltpu.VMEM((27, 64, 128), BF),
            pltpu.VMEM((128, 1024), BF),
            pltpu.VMEM((128, 1024), BF),
            pltpu.VMEM((16, 32, LANES), BF),
            pltpu.VMEM((16, 32, LANES), BF),
            pltpu.VMEM((10, 288, 1024), BF),
            pltpu.VMEM((10, 192, 1024), F32),
            pltpu.VMEM((8, 64, 1024), BF),
            pltpu.VMEM((192, 288), BF),
            pltpu.VMEM((1024, 512), BF),
            pltpu.VMEM((16, 32, LANES), BF),
            pltpu.VMEM((16, 32, LANES), BF),
            pltpu.VMEM((384, 576), BF),
            pltpu.VMEM((192, 1152), BF),
            pltpu.VMEM((576, 1024), BF),
            pltpu.VMEM((384, 1024), BF),
            pltpu.VMEM((1152, 1024), BF),
            pltpu.VMEM((576, 384), F32),
            pltpu.VMEM((16, 32, LANES), BF),
            pltpu.VMEM((16, 32, LANES), BF),
            pltpu.VMEM((512, LANES), BF),
            pltpu.VMEM((12, 64, 1024), BF),
            pltpu.VMEM((288, 256), F32),
            dma((5,)), dma((2,)), dma((2,)), dma((15,)), dma((15,)), dma((15,)), dma((15,)),
        ]
        + Sum.scratch(TILES1, ROWS1, F32)
        + Sum.scratch(TILES2, ROWS2, BF),
        compiler_params=pltpu.CompilerParams(
            vmem_limit_bytes=56 << 20, collective_id=0, has_side_effects=True
        ),
    )(
        volumes, jnp.swapaxes(kernel_first, 1, 2), bias_first.reshape(1, -1),
        jnp.swapaxes(kernel_second, 1, 2), bias_second.reshape(1, -1), grad_out,
    )
    taps1 = jnp.swapaxes(out1 * scale_one, 1, 2)
    taps2 = out2.reshape(-1, LANES)[: 27 * 64].astype(F32) * scale_two
    taps2 = jnp.swapaxes(taps2.reshape(27, 64, LANES), 1, 2)
    return feat, taps1, outb[0, :64] * scale_one, taps2, outb[1] * scale_two


def solution(mesh):
    in_specs = (P("sample", None, "space"), P(("sample", "space"), None, None), P(), P(), P(), P())
    out_specs = (P(("sample", "space"), None, None), P(), P(), P(), P())
    return jax.shard_map(
        on_device, mesh=mesh, in_specs=in_specs, out_specs=out_specs, check_vma=False
    )
```

```python
import functools
import math

import jax
import jax.numpy as jnp
from jax import lax
from jax.experimental import pallas as pl
from jax.experimental.pallas import tpu as pltpu
from jax.sharding import PartitionSpec as P

LEAK_SLOPE = 0.3
BF = jnp.bfloat16
F32 = jnp.float32
MESH = pl.DeviceIdType.MESH
LANES = 128
PARTS = 8
TILES1, ROWS1 = 7, 8
TILES2, ROWS2 = 14, 16


def lane_iota(rows):
    return lax.broadcasted_iota(jnp.int32, (rows, LANES), 1)


def dot(a, b, ca=1, cb=0):
    return lax.dot_general(a, b, (((ca,), (cb,)), ((), ())), preferred_element_type=F32)


def column(row, n):
    r = lax.broadcasted_iota(jnp.int32, (n, n), 0)
    c = lax.broadcasted_iota(jnp.int32, (n, n), 1)
    return jnp.sum(jnp.where(r == c, jnp.broadcast_to(row, (n, n)), 0.0), axis=1, keepdims=True)


def row_of(col, n):
    r = lax.broadcasted_iota(jnp.int32, (n, n), 0)
    c = lax.broadcasted_iota(jnp.int32, (n, n), 1)
    return jnp.sum(jnp.where(r == c, jnp.broadcast_to(col, (n, n)), 0.0), axis=0, keepdims=True)


def tap_masks(rows, side, mirror):
    lane = lane_iota(rows)
    h = (lane // side) % side
    w = lane % side
    out = []
    for t in range(9):
        dh, dw = t // 3 - 1, t % 3 - 1
        if mirror:
            dh, dw = -dh, -dw
        ok = (h + dh >= 0) & (h + dh < side) & (w + dw >= 0) & (w + dw < side)
        mask = jnp.where(ok, 1.0, 0.0).astype(BF) if (dh or dw) else None
        out.append((mask, (-(dh * side + dw)) % LANES))
    return out


def taps_of(x, masks):
    return [x if m is None else pltpu.roll(x, s, 1) * m for m, s in masks]


def pool_matrix(value, transpose):
    shape = (LANES, 4 * LANES) if transpose else (4 * LANES, LANES)
    big = lax.broadcasted_iota(jnp.int32, shape, 1 if transpose else 0)
    small = lax.broadcasted_iota(jnp.int32, shape, 0 if transpose else 1)
    q, lane = big // LANES, big % LANES
    target = (lane // 64) * 64 + q * 16 + ((lane % 64) // 16) * 4 + (lane % 8) // 2
    return jnp.where(target == small, value, 0.0).astype(BF)


def split_pair(pair, lo):
    top, bottom = pair[:32], pair[32:]
    return (
        jnp.where(lo, top, pltpu.roll(bottom, 64, 1)),
        jnp.where(lo, pltpu.roll(top, 64, 1), bottom),
    )


def join_pair(first, second, lo):
    return (
        jnp.where(lo, first, pltpu.roll(second, 64, 1)),
        jnp.where(lo, pltpu.roll(first, 64, 1), second),
    )


def position():
    sample, space = lax.axis_index("sample"), lax.axis_index("space")
    core = sample % 2
    y = (sample // 2) % 8
    z = (sample // 16) * 4 + space // 4
    x = space % 4
    return core, x, y, z


def device(core, x, y, z):
    return ((z // 4) * 16 + y * 2 + core, (z % 4) * 4 + x)


def space_peers():
    sample, space = lax.axis_index("sample"), lax.axis_index("space")
    return [(sample, (space + k) % 16) for k in range(1, 16)]


def all_peers():
    core, x, y, z = position()
    out = space_peers()
    out += [device(core, x, (y + k) % 8, z) for k in range(1, 8)]
    out += [device(core, x, y, (1 - z // 4) * 4 + k) for k in range(4)]
    out += [device(1 - core, x, y, z)]
    return out


def remote(src, dst, ssem, rsem, peer):
    return pltpu.make_async_remote_copy(
        src_ref=src, dst_ref=dst, send_sem=ssem, recv_sem=rsem,
        device_id=peer, device_id_type=MESH,
    )


def exchange(send, recv, ssem, rsem):
    me = lax.axis_index("space")
    copies = []
    for k, peer in enumerate(space_peers()):
        copy = remote(send.at[peer[1]], recv.at[me], ssem.at[k], rsem.at[k], peer)
        copy.start()
        copies.append(copy)
    recv[me] = send[me]
    return copies


class Sum:
    def __init__(self, tiles, rows, kind, refs):
        self.tiles, self.rows, self.kind = tiles, rows, kind
        self.share = -(-tiles // 8)
        (self.g, self.rc, self.xs, self.rx, self.ys, self.ry, self.rz, self.fs, self.ay, self.bx,
         self.out, self.ssem, self.rsem) = refs
        self.pos = core, x, y, z = position()
        self.other = device(1 - core, x, y, z)
        self.xp = [device(core, (x + k) % 4, y, z) for k in range(1, 4)]
        self.yp = [device(core, x, (y + k) % 8, z) for k in range(1, 8)]
        self.zp = [device(core, x, y, (z + k) % 8) for k in range(1, 8)]
        self.started, self.now = [], []

    @staticmethod
    def scratch(tiles, rows, kind):
        share = -(-tiles // 8)
        dims = [
            (PARTS, tiles), (4, tiles), (4, tiles), (3, tiles), (8 * share,), (7, share),
            (8, share), (share,), (8 * share,), (4, tiles), (PARTS, tiles),
        ]
        out = [pltpu.VMEM(d + (rows, LANES), kind) for d in dims]
        return out + [pltpu.SemaphoreType.DMA((29,)), pltpu.SemaphoreType.DMA((29,))]

    def send(self, i, src, dst, peer):
        copy = remote(src, dst, self.ssem.at[i], self.rsem.at[i], peer)
        copy.start()
        self.started.append(copy)
        self.now.append(copy)

    def arrive(self):
        for copy in self.now:
            copy.wait_recv()
        self.now = []

    def mine(self, ref):
        return ref.at[pl.ds(self.pos[2] * self.share, self.share)]

    def step(self, i):
        core, x, y, z = self.pos
        kind = self.kind
        if i == 0:
            self.send(0, self.g.at[pl.ds((1 - core) * 4, 4)], self.rc, self.other)
            return
        self.arrive()
        if i == 1:
            for n in range(4):
                self.xs[n] = (self.g[core * 4 + n].astype(F32) + self.rc[n].astype(F32)).astype(kind)
            for k in range(3):
                self.send(1 + k, self.xs.at[(x + k + 1) % 4], self.rx.at[k], self.xp[k])
        elif i == 2:
            total = self.xs[x].astype(F32)
            for k in range(3):
                total = total + self.rx[k].astype(F32)
            self.ys[0 : self.tiles] = total.astype(kind)
            for k in range(7):
                at = pl.ds(((y + k + 1) % 8) * self.share, self.share)
                self.send(4 + k, self.ys.at[at], self.ry.at[k], self.yp[k])
        elif i == 3:
            total = self.ys[pl.ds(y * self.share, self.share)].astype(F32)
            for k in range(7):
                total = total + self.ry[k].astype(F32)
            self.fs[...] = total.astype(kind)
            self.rz[z] = total.astype(kind)
            for k in range(7):
                self.send(11 + k, self.fs, self.rz.at[z], self.zp[k])
        elif i == 4:
            total = self.rz[0].astype(F32)
            for k in range(1, 8):
                total = total + self.rz[k].astype(F32)
            self.ay[pl.ds(y * self.share, self.share)] = total.astype(kind)
            for k in range(7):
                self.send(18 + k, self.mine(self.ay), self.mine(self.ay), self.yp[k])
        elif i == 5:
            for k in range(3):
                self.send(25 + k, self.ay.at[0 : self.tiles], self.bx.at[x], self.xp[k])
            self.bx[x] = self.ay[0 : self.tiles]
        elif i == 6:
            self.send(28, self.bx, self.out.at[pl.ds(core * 4, 4)], self.other)
            for n in range(4):
                self.out[core * 4 + n] = self.bx[n]

    def finish(self):
        for copy in self.started:
            copy.wait_send()


def put_taps(x, masks, s9, s, j):
    for t, y in enumerate(taps_of(x, masks)):
        s9[s, 32 * t : 32 * t + 32, LANES * j : LANES * j + LANES] = y


def inner_taps(vol, s9, masks, lo):
    @pl.loop(0, 4)
    def _(t):
        at = pl.ds(pl.multiple_of(t * LANES, LANES), LANES)
        for j in range(8):
            a, b = vol[2 * j, :, at], vol[2 * j + 1, :, at]
            put_taps(jnp.where(lo, a, pltpu.roll(b, 64, 1)), masks, s9, 2 * t + 1, j)
            put_taps(jnp.where(lo, pltpu.roll(a, 64, 1), b), masks, s9, 2 * t + 2, j)


def outer_taps(before, after, s9, masks, lo):
    for j in range(8):
        a, b = before[2 * j], before[2 * j + 1]
        put_taps(jnp.where(lo, pltpu.roll(a, 64, 1), b), masks, s9, 0, j)
        a, b = after[2 * j], after[2 * j + 1]
        put_taps(jnp.where(lo, a, pltpu.roll(b, 64, 1)), masks, s9, 9, j)


def first_outputs(part, b1, keep, yb, send, lo):
    bias = column(b1[...], 64)

    @pl.loop(0, 4)
    def _(q):
        total = None
        for r in range(2):
            p = 2 * q + r
            pre = part[p, 0:64] + part[p + 1, 64:128] + part[p + 2, 128:192] + bias
            positive = pre > 0
            keep[p] = jnp.where(positive, 1.0, 0.0).astype(BF)
            act = jnp.where(positive, pre, LEAK_SLOPE * pre)
            total = act if total is None else total + act
        high = total.astype(BF)
        low = (total - high.astype(F32)).astype(BF)
        at = pl.ds(pl.multiple_of(q * LANES, LANES), LANES)
        for j in range(8):
            cut = slice(LANES * j, LANES * j + LANES)
            yb[LANES * j : LANES * j + 64, at] = high[:, cut]
            yb[LANES * j + 64 : LANES * j + LANES, at] = low[:, cut]

    z = dot(yb[...], pool_matrix(0.125, False))
    for j in range(8):
        pooled = z[LANES * j : LANES * j + 64] + z[LANES * j + 64 : LANES * j + LANES]
        one, two = split_pair(pooled, lo)
        send[2 * j] = one.astype(BF)
        send[2 * j + 1] = two.astype(BF)


def shift_planes(x, by):
    lane = lax.broadcasted_iota(jnp.int32, x.shape, 1)
    zero = jnp.zeros_like(x)
    if by > 0:
        return jnp.where(lane < 16, zero, pltpu.roll(x, 16, 1))
    return jnp.where(lane >= 1008, zero, pltpu.roll(x, 1008, 1))


def second_layer(recv, w2, wb, b2, grad, features, send, d3, s9b, d9, lo):
    forward = tap_masks(64, 4, False)
    for i in range(8):
        cut = slice(LANES * i, LANES * i + LANES)
        top, bottom = join_pair(recv[2 * i], recv[2 * i + 1], lo)
        x = jnp.concatenate([top, bottom], axis=0)
        for t, y in enumerate(taps_of(x, forward)):
            s9b[64 * t : 64 * t + 64, cut] = y
    p3 = dot(w2[...], s9b[...])
    second = shift_planes(p3[0:128], 1) + p3[128:256] + shift_planes(p3[256:384], -1)
    second = second + column(b2[...], 128)
    positive = second > 0
    features[...] = jnp.where(positive, second, LEAK_SLOPE * second).astype(BF)
    delta = (grad[...].astype(F32) * jnp.where(positive, 1.0, LEAK_SLOPE)).astype(BF)
    d3[128:256] = delta

    backward = tap_masks(128, 4, True)
    for i in range(8):
        cut = slice(LANES * i, LANES * i + LANES)
        for t, y in enumerate(taps_of(delta[:, cut], backward)):
            d9[128 * t : 128 * t + 128, cut] = y
    r3 = dot(wb[...], d9[...])
    spread = shift_planes(r3[0:64], -1) + r3[64:128] + shift_planes(r3[128:192], 1)
    for i in range(8):
        one, two = split_pair(spread[:, LANES * i : LANES * i + LANES], lo)
        send[2 * i] = one.astype(BF)
        send[2 * i + 1] = two.astype(BF)


def second_taps(d3, s9b, acc2, g2):
    delta = d3[128:256]
    d3[0:128] = shift_planes(delta, -1)
    d3[256:384] = shift_planes(delta, 1)
    acc2[...] = dot(s9b[...], d3[...], 1, 1)
    for a in range(3):
        for r in range(36):
            t = 36 * a + r
            tile = acc2[16 * r : 16 * r + 16, LANES * a : LANES * a + LANES]
            g2[t // TILES2, t % TILES2] = tile.astype(BF)
    for t in range(108, PARTS * TILES2):
        g2[t // TILES2, t % TILES2] = jnp.zeros((ROWS2, LANES), BF)
    return row_of(jnp.sum(delta.astype(F32), axis=1, keepdims=True), 128)


def first_deltas(recv, keep, tt, dr, lo):
    for j in range(8):
        top, bottom = join_pair(recv[2 * j], recv[2 * j + 1], lo)
        tt[64 * j : 64 * j + 32] = top
        tt[64 * j + 32 : 64 * j + 64] = bottom
    for i in (0, 1, 10, 11):
        dr[i] = jnp.zeros((64, 1024), BF)
    spread_to = pool_matrix(1.0, True)
    total = jnp.zeros((64, LANES), F32)
    for q in range(4):
        u = dot(tt[...], spread_to[:, LANES * q : LANES * q + LANES])
        for r in range(2):
            p = 2 * q + r
            for j in range(8):
                cut = slice(LANES * j, LANES * j + LANES)
                slope = jnp.where(keep[p, :, cut] > 0, 1.0, LEAK_SLOPE).astype(F32)
                delta = (u[64 * j : 64 * j + 64] * 0.125 * slope).astype(BF)
                dr[9 - p, :, cut] = delta
                total = total + delta.astype(F32)
    return row_of(jnp.sum(total, axis=1, keepdims=True), 64)


def first_taps(s9, dr, acc1, first, last):
    acc = None
    for s in range(first, last):
        term = dot(s9[s], dr[9 - s : 12 - s].reshape(192, 1024), 1, 1)
        acc = term if acc is None else acc + term
    if first == 0:
        acc1[:, 0:192] = acc
    else:
        acc1[:, 0:192] += acc


def pack_first(acc1, bias1, bias2, g1):
    lo = lane_iota(8) < 64
    row = lax.broadcasted_iota(jnp.int32, (8, LANES), 0)

    def put(t, value):
        g1[t // TILES1, t % TILES1] = value

    for k in range(36):
        put(k, acc1[8 * k : 8 * k + 8, 0:LANES])
    for k in range(18):
        left = acc1[8 * k : 8 * k + 8, LANES:256]
        right = acc1[144 + 8 * k : 152 + 8 * k, LANES:256]
        put(36 + k, jnp.where(lo, left, pltpu.roll(right, 64, 1)))
    one = jnp.concatenate([bias1, jnp.zeros((1, 64), F32)], axis=1)
    one = jnp.broadcast_to(one, (8, LANES))
    two = jnp.broadcast_to(bias2, (8, LANES))
    put(54, jnp.where(row == 0, one, jnp.where(row == 1, two, 0.0)))
    put(55, jnp.zeros((8, LANES), F32))


def finish_kernel(
    scale_one, scale_two, feat_in, c1_in, c2_in, feat_out, out1, out2, outb1, outb2, feat, c1, c2, sem
):
    loads = [
        pltpu.make_async_copy(src, dst, sem.at[i])
        for i, (src, dst) in enumerate(((c2_in, c2), (c1_in, c1), (feat_in, feat)))
    ]
    for load in loads:
        load.start()
    loads[0].wait()

    def get(t):
        return c1[t // TILES1, t % TILES1] * scale_one

    def put(a, r, value):
        out1[9 * a + r // 4, 8 * (r % 4) : 8 * (r % 4) + 8] = value

    for t in range(108):
        tile = c2[t // TILES2, t % TILES2].astype(F32) * scale_two
        out2[t // 4, 16 * (t % 4) : 16 * (t % 4) + 16] = tile
    loads[1].wait()
    for k in range(36):
        tile = get(k)
        put(0, k, tile[:, 0:64])
        put(1, k, tile[:, 64:128])
    for k in range(18):
        tile = get(36 + k)
        put(2, k, tile[:, 0:64])
        put(2, 18 + k, tile[:, 64:128])
    tile = c1[54 // TILES1, 54 % TILES1]
    outb1[...] = tile[0:1, 0:64] * scale_one
    outb2[...] = tile[1:2] * scale_two
    loads[2].wait()
    feat_out[0] = feat[...]


def step_kernel(
    vol_in, k1_in, b1, k2_in, b2, grad_in, feat_out, out1, out2,
    vol, k1, k2, grad, feat, before, after, s9, part, keep, w1, yb, send1, recv1,
    w2, wb, s9b, d3, d9, acc2, send2, recv2, tt, dr, acc1,
    lsem, hssem, hrsem, s1, r1, s2, r2, *sums,
):
    space = lax.axis_index("space")
    sample = lax.axis_index("sample")
    n = len(sums) // 2
    sum1 = Sum(TILES1, ROWS1, F32, sums[:n])
    sum2 = Sum(TILES2, ROWS2, BF, sums[n:])
    peers = all_peers()
    barrier = pltpu.get_barrier_semaphore()
    for peer in peers:
        pl.semaphore_signal(barrier, inc=1, device_id=peer, device_id_type=MESH)
    loads = [
        pltpu.make_async_copy(src, dst, lsem.at[i])
        for i, (src, dst) in enumerate(((vol_in, vol), (k1_in, k1), (k2_in, k2), (grad_in.at[0], grad)))
    ]
    for load in loads:
        load.start()

    lo = lane_iota(32) < 64
    masks = tap_masks(32, 8, False)
    loads[0].wait()
    inner_taps(vol, s9, masks, lo)
    loads[1].wait()
    for a in range(3):
        w1[64 * a : 64 * a + 64] = jnp.transpose(k1[9 * a : 9 * a + 9].reshape(288, 64))

    pl.semaphore_wait(barrier, len(peers))
    tail = remote(vol.at[:, :, pl.ds(384, 128)], before, hssem.at[0], hrsem.at[0], (sample, (space + 1) % 16))
    head = remote(vol.at[:, :, pl.ds(0, 128)], after, hssem.at[1], hrsem.at[1], (sample, (space + 15) % 16))

    @pl.when(space < 15)
    def _():
        tail.start()

    @pl.when(space > 0)
    def _():
        head.start()

    @pl.when(space == 0)
    def _():
        before[...] = jnp.zeros_like(before)

    @pl.when(space == 15)
    def _():
        after[...] = jnp.zeros_like(after)

    for s in range(1, 9):
        part[s] = dot(w1[...], s9[s])

    @pl.when(space > 0)
    def _():
        tail.wait_recv()
        head.wait_send()

    @pl.when(space < 15)
    def _():
        head.wait_recv()
        tail.wait_send()

    outer_taps(before, after, s9, masks, lo)
    for s in (0, 9):
        part[s] = dot(w1[...], s9[s])
    first_outputs(part, b1, keep, yb, send1, lo)
    there = exchange(send1, recv1, s1, r1)

    loads[2].wait()
    for a in range(3):
        w2[128 * a : 128 * a + 128] = jnp.transpose(k2[9 * a : 9 * a + 9].reshape(576, 128))
        for t in range(9):
            wb[64 * a : 64 * a + 64, 128 * t : 128 * t + 128] = k2[9 * a + t]
    loads[3].wait()
    for copy in there:
        copy.wait_recv()
    second_layer(recv1, w2, wb, b2, grad, feat, send2, d3, s9b, d9, lo)
    back = exchange(send2, recv2, s2, r2)

    writes = [
        pltpu.make_async_copy(src, dst, lsem.at[4 + i])
        for i, (src, dst) in enumerate(((feat, feat_out), (sum2.out, out2), (sum1.out, out1)))
    ]
    writes[0].start()

    bias2 = second_taps(d3, s9b, acc2, sum2.g)
    for total in (sum1, sum2):
        pad = 8 * total.share - total.tiles
        total.ys[total.tiles : 8 * total.share] = jnp.zeros((pad, total.rows, LANES), total.kind)
    sum2.step(0)
    sum2.step(1)
    for copy in back:
        copy.wait_recv()
    bias1 = first_deltas(recv2, keep, tt, dr, lo)
    first_taps(s9, dr, acc1, 0, 7)
    sum2.step(2)
    first_taps(s9, dr, acc1, 7, 10)
    pack_first(acc1, bias1, bias2, sum1.g)
    sum1.step(0)
    sum1.step(1)
    sum2.step(3)
    sum1.step(2)
    sum2.step(4)
    sum1.step(3)
    sum2.step(5)
    sum1.step(4)
    sum2.step(6)
    sum1.step(5)
    sum2.step(7)
    writes[1].start()
    sum1.step(6)
    sum1.step(7)
    writes[2].start()
    for copy in there + back:
        copy.wait_send()
    sum1.finish()
    sum2.finish()
    for write in writes:
        write.wait()


def shape(dims, kind=BF):
    return jax.ShapeDtypeStruct(dims, kind)


def on_device(volumes, grad_out, kernel_first, bias_first, kernel_second, bias_second):
    devices = lax.axis_size("sample") * lax.axis_size("space")
    scale_one = 1.0 / math.sqrt(volumes.shape[0] * volumes.shape[2] * devices)
    scale_two = 1.0 / math.sqrt(grad_out.shape[0] * grad_out.shape[2] * devices)
    vmem = pl.BlockSpec(memory_space=pltpu.VMEM)
    anywhere = pl.BlockSpec(memory_space=pltpu.HBM)
    dma = pltpu.SemaphoreType.DMA
    feat, sums1, sums2 = pl.pallas_call(
        step_kernel,
        name="step",
        out_shape=[
            shape((128, 1024)), shape((PARTS, TILES1, ROWS1, LANES), F32),
            shape((PARTS, TILES2, ROWS2, LANES)),
        ],
        in_specs=[anywhere, anywhere, vmem, anywhere, vmem, anywhere],
        out_specs=[anywhere] * 3,
        scratch_shapes=[
            pltpu.VMEM((16, 32, 512), BF),
            pltpu.VMEM((27, 32, 64), BF),
            pltpu.VMEM((27, 64, 128), BF),
            pltpu.VMEM((128, 1024), BF),
            pltpu.VMEM((128, 1024), BF),
            pltpu.VMEM((16, 32, LANES), BF),
            pltpu.VMEM((16, 32, LANES), BF),
            pltpu.VMEM((10, 288, 1024), BF),
            pltpu.VMEM((10, 192, 1024), F32),
            pltpu.VMEM((8, 64, 1024), BF),
            pltpu.VMEM((192, 288), BF),
            pltpu.VMEM((1024, 512), BF),
            pltpu.VMEM((16, 32, LANES), BF),
            pltpu.VMEM((16, 32, LANES), BF),
            pltpu.VMEM((384, 576), BF),
            pltpu.VMEM((192, 1152), BF),
            pltpu.VMEM((576, 1024), BF),
            pltpu.VMEM((384, 1024), BF),
            pltpu.VMEM((1152, 1024), BF),
            pltpu.VMEM((576, 384), F32),
            pltpu.VMEM((16, 32, LANES), BF),
            pltpu.VMEM((16, 32, LANES), BF),
            pltpu.VMEM((512, LANES), BF),
            pltpu.VMEM((12, 64, 1024), BF),
            pltpu.VMEM((288, 256), F32),
            dma((7,)), dma((2,)), dma((2,)), dma((15,)), dma((15,)), dma((15,)), dma((15,)),
        ]
        + Sum.scratch(TILES1, ROWS1, F32)
        + Sum.scratch(TILES2, ROWS2, BF),
        compiler_params=pltpu.CompilerParams(
            vmem_limit_bytes=56 << 20, collective_id=0, has_side_effects=True
        ),
    )(
        volumes, jnp.swapaxes(kernel_first, 1, 2), bias_first.reshape(1, -1),
        jnp.swapaxes(kernel_second, 1, 2), bias_second.reshape(1, -1), grad_out,
    )
    feat, out1, out2, outb1, outb2 = pl.pallas_call(
        functools.partial(finish_kernel, scale_one, scale_two),
        name="finish",
        out_shape=[
            shape((1, 128, 1024)), shape((27, 32, 64), F32), shape((27, 64, 128), F32),
            shape((1, 64), F32), shape((1, 128), F32),
        ],
        in_specs=[anywhere] * 3,
        out_specs=[vmem] * 5,
        scratch_shapes=[
            pltpu.VMEM((128, 1024), BF),
            pltpu.VMEM((PARTS, TILES1, ROWS1, LANES), F32),
            pltpu.VMEM((PARTS, TILES2, ROWS2, LANES), BF),
            dma((3,)),
        ],
        compiler_params=pltpu.CompilerParams(vmem_limit_bytes=56 << 20),
    )(feat, sums1, sums2)
    out1, out2 = jnp.swapaxes(out1, 1, 2), jnp.swapaxes(out2, 1, 2)
    return feat, out1, outb1.reshape(-1), out2, outb2.reshape(-1)


def solution(mesh):
    in_specs = (P("sample", None, "space"), P(("sample", "space"), None, None), P(), P(), P(), P())
    out_specs = (P(("sample", "space"), None, None), P(), P(), P(), P())
    return jax.shard_map(
        on_device, mesh=mesh, in_specs=in_specs, out_specs=out_specs, check_vma=False
    )
```

```python
import functools
import math

import jax
import jax.numpy as jnp
from jax import lax
from jax.experimental import pallas as pl
from jax.experimental.pallas import tpu as pltpu
from jax.sharding import PartitionSpec as P

LEAK_SLOPE = 0.3
BF = jnp.bfloat16
F32 = jnp.float32
MESH = pl.DeviceIdType.MESH
LANES = 128
PARTS = 8
OTHER_TAPS = (0, 1, 2, 3, 5, 6, 7, 8)
TILES1, ROWS1 = 7, 8
TILES2, ROWS2 = 14, 16


def lane_iota(rows):
    return lax.broadcasted_iota(jnp.int32, (rows, LANES), 1)


def dot(a, b, ca=1, cb=0):
    return lax.dot_general(a, b, (((ca,), (cb,)), ((), ())), preferred_element_type=F32)


def column(row, n):
    r = lax.broadcasted_iota(jnp.int32, (n, n), 0)
    c = lax.broadcasted_iota(jnp.int32, (n, n), 1)
    return jnp.sum(jnp.where(r == c, jnp.broadcast_to(row, (n, n)), 0.0), axis=1, keepdims=True)


def row_of(col, n):
    r = lax.broadcasted_iota(jnp.int32, (n, n), 0)
    c = lax.broadcasted_iota(jnp.int32, (n, n), 1)
    return jnp.sum(jnp.where(r == c, jnp.broadcast_to(col, (n, n)), 0.0), axis=0, keepdims=True)


def tap_masks(rows, side, mirror):
    lane = lane_iota(rows)
    h = (lane // side) % side
    w = lane % side
    out = []
    for t in range(9):
        dh, dw = t // 3 - 1, t % 3 - 1
        if mirror:
            dh, dw = -dh, -dw
        ok = (h + dh >= 0) & (h + dh < side) & (w + dw >= 0) & (w + dw < side)
        mask = jnp.where(ok, 1.0, 0.0).astype(BF) if (dh or dw) else None
        out.append((mask, (-(dh * side + dw)) % LANES))
    return out


def taps_of(x, masks):
    return [x if m is None else pltpu.roll(x, s, 1) * m for m, s in masks]


def pool_matrix(value, transpose):
    shape = (LANES, 4 * LANES) if transpose else (4 * LANES, LANES)
    big = lax.broadcasted_iota(jnp.int32, shape, 1 if transpose else 0)
    small = lax.broadcasted_iota(jnp.int32, shape, 0 if transpose else 1)
    q, lane = big // LANES, big % LANES
    target = (lane // 64) * 64 + q * 16 + ((lane % 64) // 16) * 4 + (lane % 8) // 2
    return jnp.where(target == small, value, 0.0).astype(BF)


def split_pair(pair, lo):
    top, bottom = pair[:32], pair[32:]
    return (
        jnp.where(lo, top, pltpu.roll(bottom, 64, 1)),
        jnp.where(lo, pltpu.roll(top, 64, 1), bottom),
    )


def join_pair(first, second, lo):
    return (
        jnp.where(lo, first, pltpu.roll(second, 64, 1)),
        jnp.where(lo, pltpu.roll(first, 64, 1), second),
    )


def position():
    sample, space = lax.axis_index("sample"), lax.axis_index("space")
    core = sample % 2
    y = (sample // 2) % 8
    z = (sample // 16) * 4 + space // 4
    x = space % 4
    return core, x, y, z


def device(core, x, y, z):
    return ((z // 4) * 16 + y * 2 + core, (z % 4) * 4 + x)


def space_peers():
    sample, space = lax.axis_index("sample"), lax.axis_index("space")
    return [(sample, (space + k) % 16) for k in range(1, 16)]


def all_peers():
    core, x, y, z = position()
    out = space_peers()
    out += [device(core, x, (y + k) % 8, z) for k in range(1, 8)]
    out += [device(core, x, y, (1 - z // 4) * 4 + k) for k in range(4)]
    out += [device(1 - core, x, y, z)]
    return out


def remote(src, dst, ssem, rsem, peer):
    return pltpu.make_async_remote_copy(
        src_ref=src, dst_ref=dst, send_sem=ssem, recv_sem=rsem,
        device_id=peer, device_id_type=MESH,
    )


def exchange(send, recv, ssem, rsem):
    me = lax.axis_index("space")
    copies = []
    for k, peer in enumerate(space_peers()):
        copy = remote(send.at[peer[1]], recv.at[me], ssem.at[k], rsem.at[k], peer)
        copy.start()
        copies.append(copy)
    recv[me] = send[me]
    return copies


class Sum:
    def __init__(self, tiles, rows, kind, refs):
        self.tiles, self.rows, self.kind = tiles, rows, kind
        self.share = -(-tiles // 8)
        (self.g, self.rc, self.xs, self.rx, self.ys, self.ry, self.rz, self.fs, self.ay, self.bx,
         self.out, self.ssem, self.rsem) = refs
        self.pos = core, x, y, z = position()
        self.other = device(1 - core, x, y, z)
        self.xp = [device(core, (x + k) % 4, y, z) for k in range(1, 4)]
        self.yp = [device(core, x, (y + k) % 8, z) for k in range(1, 8)]
        self.zp = [device(core, x, y, (z + k) % 8) for k in range(1, 8)]
        self.started, self.now = [], []

    @staticmethod
    def scratch(tiles, rows, kind):
        share = -(-tiles // 8)
        dims = [
            (PARTS, tiles), (4, tiles), (4, tiles), (3, tiles), (8 * share,), (7, share),
            (8, share), (share,), (8 * share,), (4, tiles), (PARTS, tiles),
        ]
        out = [pltpu.VMEM(d + (rows, LANES), kind) for d in dims]
        return out + [pltpu.SemaphoreType.DMA((29,)), pltpu.SemaphoreType.DMA((29,))]

    def send(self, i, src, dst, peer):
        copy = remote(src, dst, self.ssem.at[i], self.rsem.at[i], peer)
        copy.start()
        self.started.append(copy)
        self.now.append(copy)

    def arrive(self):
        for copy in self.now:
            copy.wait_recv()
        self.now = []

    def mine(self, ref):
        return ref.at[pl.ds(self.pos[2] * self.share, self.share)]

    def step(self, i):
        core, x, y, z = self.pos
        kind = self.kind
        if i == 0:
            self.send(0, self.g.at[pl.ds((1 - core) * 4, 4)], self.rc, self.other)
            return
        self.arrive()
        if i == 1:
            for n in range(4):
                self.xs[n] = (self.g[core * 4 + n].astype(F32) + self.rc[n].astype(F32)).astype(kind)
            for k in range(3):
                self.send(1 + k, self.xs.at[(x + k + 1) % 4], self.rx.at[k], self.xp[k])
        elif i == 2:
            total = self.xs[x].astype(F32)
            for k in range(3):
                total = total + self.rx[k].astype(F32)
            self.ys[0 : self.tiles] = total.astype(kind)
            for k in range(7):
                at = pl.ds(((y + k + 1) % 8) * self.share, self.share)
                self.send(4 + k, self.ys.at[at], self.ry.at[k], self.yp[k])
        elif i == 3:
            total = self.ys[pl.ds(y * self.share, self.share)].astype(F32)
            for k in range(7):
                total = total + self.ry[k].astype(F32)
            self.fs[...] = total.astype(kind)
            self.rz[z] = total.astype(kind)
            for k in range(7):
                self.send(11 + k, self.fs, self.rz.at[z], self.zp[k])
        elif i == 4:
            total = self.rz[0].astype(F32)
            for k in range(1, 8):
                total = total + self.rz[k].astype(F32)
            self.ay[pl.ds(y * self.share, self.share)] = total.astype(kind)
            for k in range(7):
                self.send(18 + k, self.mine(self.ay), self.mine(self.ay), self.yp[k])
        elif i == 5:
            for k in range(3):
                self.send(25 + k, self.ay.at[0 : self.tiles], self.bx.at[x], self.xp[k])
            self.bx[x] = self.ay[0 : self.tiles]
        elif i == 6:
            self.send(28, self.bx, self.out.at[pl.ds(core * 4, 4)], self.other)
            for n in range(4):
                self.out[core * 4 + n] = self.bx[n]

    def finish(self):
        for copy in self.started:
            copy.wait_send()


def fill_shifts(shifts):
    source = lax.broadcasted_iota(jnp.int32, (LANES, LANES), 0)
    lane = lane_iota(LANES)
    h, w = (lane // 8) % 8, lane % 8
    for k, t in enumerate(OTHER_TAPS):
        dh, dw = t // 3 - 1, t % 3 - 1
        ok = (h + dh >= 0) & (h + dh < 8) & (w + dw >= 0) & (w + dw < 8)
        hit = ok & (source == lane + (8 * dh + dw))
        shifts[:, LANES * k : LANES * k + LANES] = jnp.where(hit, 1.0, 0.0).astype(BF)


def store_taps(rows, shifts, s9, s):
    moved = dot(rows[...], shifts[...])
    for j in range(8):
        at, cut = slice(32 * j, 32 * j + 32), slice(LANES * j, LANES * j + LANES)
        s9[s, 128:160, cut] = rows[at]
        for k, t in enumerate(OTHER_TAPS):
            s9[s, 32 * t : 32 * t + 32, cut] = moved[at, LANES * k : LANES * k + LANES].astype(BF)


def inner_taps(vol, s9, xs, shifts, lo):
    @pl.loop(0, 4)
    def _(t):
        at = pl.ds(pl.multiple_of(t * LANES, LANES), LANES)
        for j in range(8):
            a, b = vol[2 * j, :, at], vol[2 * j + 1, :, at]
            xs[0, 32 * j : 32 * j + 32] = jnp.where(lo, a, pltpu.roll(b, 64, 1))
            xs[1, 32 * j : 32 * j + 32] = jnp.where(lo, pltpu.roll(a, 64, 1), b)
        store_taps(xs.at[0], shifts, s9, 2 * t + 1)
        store_taps(xs.at[1], shifts, s9, 2 * t + 2)


def outer_taps(before, after, s9, xs, shifts, lo):
    for j in range(8):
        a, b = before[2 * j], before[2 * j + 1]
        xs[0, 32 * j : 32 * j + 32] = jnp.where(lo, pltpu.roll(a, 64, 1), b)
        a, b = after[2 * j], after[2 * j + 1]
        xs[1, 32 * j : 32 * j + 32] = jnp.where(lo, a, pltpu.roll(b, 64, 1))
    store_taps(xs.at[0], shifts, s9, 0)
    store_taps(xs.at[1], shifts, s9, 9)


def first_planes(part, b1, keep, yb, qs):
    bias = column(b1[...], 64)
    for q in qs:
        total = None
        for r in range(2):
            p = 2 * q + r
            pre = part[p, 0:64] + part[p + 1, 64:128] + part[p + 2, 128:192] + bias
            positive = pre > 0
            keep[p] = jnp.where(positive, 1.0, 0.0).astype(BF)
            act = jnp.where(positive, pre, LEAK_SLOPE * pre)
            total = act if total is None else total + act
        high = total.astype(BF)
        low = (total - high.astype(F32)).astype(BF)
        at = slice(LANES * q, LANES * q + LANES)
        for j in range(8):
            cut = slice(LANES * j, LANES * j + LANES)
            yb[LANES * j : LANES * j + 64, at] = high[:, cut]
            yb[LANES * j + 64 : LANES * j + LANES, at] = low[:, cut]


def first_outputs(yb, send, lo):
    z = dot(yb[...], pool_matrix(0.125, False))
    for j in range(8):
        pooled = z[LANES * j : LANES * j + 64] + z[LANES * j + 64 : LANES * j + LANES]
        one, two = split_pair(pooled, lo)
        send[2 * j] = one.astype(BF)
        send[2 * j + 1] = two.astype(BF)


def shift_planes(x, by):
    lane = lax.broadcasted_iota(jnp.int32, x.shape, 1)
    zero = jnp.zeros_like(x)
    if by > 0:
        return jnp.where(lane < 16, zero, pltpu.roll(x, 16, 1))
    return jnp.where(lane >= 1008, zero, pltpu.roll(x, 1008, 1))


def second_layer(recv, w2, wb, b2, grad, features, send, d3, s9b, d9, lo):
    forward = tap_masks(64, 4, False)
    for i in range(8):
        cut = slice(LANES * i, LANES * i + LANES)
        top, bottom = join_pair(recv[2 * i], recv[2 * i + 1], lo)
        x = jnp.concatenate([top, bottom], axis=0)
        for t, y in enumerate(taps_of(x, forward)):
            s9b[64 * t : 64 * t + 64, cut] = y
    p3 = dot(w2[...], s9b[...])
    second = shift_planes(p3[0:128], 1) + p3[128:256] + shift_planes(p3[256:384], -1)
    second = second + column(b2[...], 128)
    positive = second > 0
    features[...] = jnp.where(positive, second, LEAK_SLOPE * second).astype(BF)
    delta = (grad[...].astype(F32) * jnp.where(positive, 1.0, LEAK_SLOPE)).astype(BF)
    d3[128:256] = delta

    backward = tap_masks(128, 4, True)
    for i in range(8):
        cut = slice(LANES * i, LANES * i + LANES)
        for t, y in enumerate(taps_of(delta[:, cut], backward)):
            d9[128 * t : 128 * t + 128, cut] = y
    r3 = dot(wb[...], d9[...])
    spread = shift_planes(r3[0:64], -1) + r3[64:128] + shift_planes(r3[128:192], 1)
    for i in range(8):
        one, two = split_pair(spread[:, LANES * i : LANES * i + LANES], lo)
        send[2 * i] = one.astype(BF)
        send[2 * i + 1] = two.astype(BF)


def second_taps(d3, s9b, acc2, g2):
    delta = d3[128:256]
    d3[0:128] = shift_planes(delta, -1)
    d3[256:384] = shift_planes(delta, 1)
    acc2[...] = dot(s9b[...], d3[...], 1, 1)
    for a in range(3):
        for r in range(36):
            t = 36 * a + r
            tile = acc2[16 * r : 16 * r + 16, LANES * a : LANES * a + LANES]
            g2[t // TILES2, t % TILES2] = tile.astype(BF)
    for t in range(108, PARTS * TILES2):
        g2[t // TILES2, t % TILES2] = jnp.zeros((ROWS2, LANES), BF)
    return row_of(jnp.sum(delta.astype(F32), axis=1, keepdims=True), 128)


def first_deltas(recv, keep, tt, dr, lo):
    for j in range(8):
        top, bottom = join_pair(recv[2 * j], recv[2 * j + 1], lo)
        tt[64 * j : 64 * j + 32] = top
        tt[64 * j + 32 : 64 * j + 64] = bottom
    for i in (0, 1, 10, 11):
        dr[i] = jnp.zeros((64, 1024), BF)
    spread_to = pool_matrix(1.0, True)
    total = jnp.zeros((64, LANES), F32)
    for q in range(4):
        u = dot(tt[...], spread_to[:, LANES * q : LANES * q + LANES])
        for r in range(2):
            p = 2 * q + r
            for j in range(8):
                cut = slice(LANES * j, LANES * j + LANES)
                slope = jnp.where(keep[p, :, cut] > 0, 1.0, LEAK_SLOPE).astype(F32)
                delta = (u[64 * j : 64 * j + 64] * 0.125 * slope).astype(BF)
                dr[9 - p, :, cut] = delta
                total = total + delta.astype(F32)
    return row_of(jnp.sum(total, axis=1, keepdims=True), 64)


def first_taps(s9, dr, acc1, first, last):
    acc = None
    for s in range(first, last):
        term = dot(s9[s], dr[9 - s : 12 - s].reshape(192, 1024), 1, 1)
        acc = term if acc is None else acc + term
    if first == 0:
        acc1[:, 0:192] = acc
    else:
        acc1[:, 0:192] += acc


def pack_first(acc1, bias1, bias2, g1):
    lo = lane_iota(8) < 64
    row = lax.broadcasted_iota(jnp.int32, (8, LANES), 0)

    def put(t, value):
        g1[t // TILES1, t % TILES1] = value

    for k in range(36):
        put(k, acc1[8 * k : 8 * k + 8, 0:LANES])
    for k in range(18):
        left = acc1[8 * k : 8 * k + 8, LANES:256]
        right = acc1[144 + 8 * k : 152 + 8 * k, LANES:256]
        put(36 + k, jnp.where(lo, left, pltpu.roll(right, 64, 1)))
    one = jnp.concatenate([bias1, jnp.zeros((1, 64), F32)], axis=1)
    one = jnp.broadcast_to(one, (8, LANES))
    two = jnp.broadcast_to(bias2, (8, LANES))
    put(54, jnp.where(row == 0, one, jnp.where(row == 1, two, 0.0)))
    put(55, jnp.zeros((8, LANES), F32))


def finish_kernel(
    scale_one, scale_two, feat_in, c1_in, c2_in, feat_out, out1, out2, outb1, outb2, feat, c1, c2, sem
):
    loads = [
        pltpu.make_async_copy(src, dst, sem.at[i])
        for i, (src, dst) in enumerate(((c2_in, c2), (c1_in, c1), (feat_in, feat)))
    ]
    for load in loads:
        load.start()
    loads[0].wait()

    def get(t):
        return c1[t // TILES1, t % TILES1] * scale_one

    def put(a, r, value):
        out1[9 * a + r // 4, 8 * (r % 4) : 8 * (r % 4) + 8] = value

    for t in range(108):
        tile = c2[t // TILES2, t % TILES2].astype(F32) * scale_two
        out2[t // 4, 16 * (t % 4) : 16 * (t % 4) + 16] = tile
    loads[1].wait()
    for k in range(36):
        tile = get(k)
        put(0, k, tile[:, 0:64])
        put(1, k, tile[:, 64:128])
    for k in range(18):
        tile = get(36 + k)
        put(2, k, tile[:, 0:64])
        put(2, 18 + k, tile[:, 64:128])
    tile = c1[54 // TILES1, 54 % TILES1]
    outb1[...] = tile[0:1, 0:64] * scale_one
    outb2[...] = tile[1:2] * scale_two
    loads[2].wait()
    feat_out[0] = feat[...]


def step_kernel(
    vol_in, k1_in, b1_in, k2_in, b2_in, grad_in, feat_out, out1, out2,
    vol, xs, shifts, b1, b2, k1, k2, grad, feat, before, after, s9, part, keep, w1, yb, send1, recv1,
    w2, wb, s9b, d3, d9, acc2, send2, recv2, tt, dr, acc1,
    lsem, hssem, hrsem, s1, r1, s2, r2, *sums,
):
    space = lax.axis_index("space")
    sample = lax.axis_index("sample")
    n = len(sums) // 2
    sum1 = Sum(TILES1, ROWS1, F32, sums[:n])
    sum2 = Sum(TILES2, ROWS2, BF, sums[n:])
    peers = all_peers()
    barrier = pltpu.get_barrier_semaphore()
    for peer in peers:
        pl.semaphore_signal(barrier, inc=1, device_id=peer, device_id_type=MESH)
    loads = [
        pltpu.make_async_copy(src, dst, lsem.at[i])
        for i, (src, dst) in enumerate((
            (vol_in, vol), (k1_in, k1), (k2_in, k2), (grad_in.at[0], grad), (b1_in, b1), (b2_in, b2),
        ))
    ]
    for load in loads:
        load.start()

    lo = lane_iota(32) < 64
    fill_shifts(shifts)
    loads[0].wait()
    inner_taps(vol, s9, xs, shifts, lo)

    pl.semaphore_wait(barrier, len(peers))
    tail = remote(vol.at[:, :, pl.ds(384, 128)], before, hssem.at[0], hrsem.at[0], (sample, (space + 1) % 16))
    head = remote(vol.at[:, :, pl.ds(0, 128)], after, hssem.at[1], hrsem.at[1], (sample, (space + 15) % 16))

    @pl.when(space < 15)
    def _():
        tail.start()

    @pl.when(space > 0)
    def _():
        head.start()

    @pl.when(space == 0)
    def _():
        before[...] = jnp.zeros_like(before)

    @pl.when(space == 15)
    def _():
        after[...] = jnp.zeros_like(after)

    loads[1].wait()
    loads[4].wait()
    for a in range(3):
        w1[64 * a : 64 * a + 64] = jnp.transpose(k1[9 * a : 9 * a + 9].reshape(288, 64))
    for s in range(1, 9):
        part[s] = dot(w1[...], s9[s])
    first_planes(part, b1, keep, yb, (1, 2))

    @pl.when(space > 0)
    def _():
        tail.wait_recv()
        head.wait_send()

    @pl.when(space < 15)
    def _():
        head.wait_recv()
        tail.wait_send()

    outer_taps(before, after, s9, xs, shifts, lo)
    for s in (0, 9):
        part[s] = dot(w1[...], s9[s])
    first_planes(part, b1, keep, yb, (0, 3))
    first_outputs(yb, send1, lo)
    there = exchange(send1, recv1, s1, r1)

    loads[2].wait()
    for a in range(3):
        w2[128 * a : 128 * a + 128] = jnp.transpose(k2[9 * a : 9 * a + 9].reshape(576, 128))
        for t in range(9):
            wb[64 * a : 64 * a + 64, 128 * t : 128 * t + 128] = k2[9 * a + t]
    loads[3].wait()
    loads[5].wait()
    for copy in there:
        copy.wait_recv()
    second_layer(recv1, w2, wb, b2, grad, feat, send2, d3, s9b, d9, lo)
    back = exchange(send2, recv2, s2, r2)

    writes = [
        pltpu.make_async_copy(src, dst, lsem.at[6 + i])
        for i, (src, dst) in enumerate(((feat, feat_out), (sum2.out, out2), (sum1.out, out1)))
    ]
    writes[0].start()

    bias2 = second_taps(d3, s9b, acc2, sum2.g)
    for total in (sum1, sum2):
        pad = 8 * total.share - total.tiles
        total.ys[total.tiles : 8 * total.share] = jnp.zeros((pad, total.rows, LANES), total.kind)
    sum2.step(0)
    sum2.step(1)
    for copy in back:
        copy.wait_recv()
    bias1 = first_deltas(recv2, keep, tt, dr, lo)
    first_taps(s9, dr, acc1, 0, 7)
    sum2.step(2)
    first_taps(s9, dr, acc1, 7, 10)
    pack_first(acc1, bias1, bias2, sum1.g)
    sum1.step(0)
    sum1.step(1)
    sum2.step(3)
    sum1.step(2)
    sum2.step(4)
    sum1.step(3)
    sum2.step(5)
    sum1.step(4)
    sum2.step(6)
    sum1.step(5)
    sum2.step(7)
    writes[1].start()
    sum1.step(6)
    sum1.step(7)
    writes[2].start()
    for copy in there + back:
        copy.wait_send()
    sum1.finish()
    sum2.finish()
    for write in writes:
        write.wait()


def shape(dims, kind=BF):
    return jax.ShapeDtypeStruct(dims, kind)


def on_device(volumes, grad_out, kernel_first, bias_first, kernel_second, bias_second):
    devices = lax.axis_size("sample") * lax.axis_size("space")
    scale_one = 1.0 / math.sqrt(volumes.shape[0] * volumes.shape[2] * devices)
    scale_two = 1.0 / math.sqrt(grad_out.shape[0] * grad_out.shape[2] * devices)
    vmem = pl.BlockSpec(memory_space=pltpu.VMEM)
    anywhere = pl.BlockSpec(memory_space=pltpu.HBM)
    dma = pltpu.SemaphoreType.DMA
    feat, sums1, sums2 = pl.pallas_call(
        step_kernel,
        name="step",
        out_shape=[
            shape((128, 1024)), shape((PARTS, TILES1, ROWS1, LANES), F32),
            shape((PARTS, TILES2, ROWS2, LANES)),
        ],
        in_specs=[anywhere] * 6,
        out_specs=[anywhere] * 3,
        scratch_shapes=[
            pltpu.VMEM((16, 32, 512), BF),
            pltpu.VMEM((2, 256, LANES), BF),
            pltpu.VMEM((LANES, 8 * LANES), BF),
            pltpu.VMEM((1, 64), F32),
            pltpu.VMEM((1, 128), F32),
            pltpu.VMEM((27, 32, 64), BF),
            pltpu.VMEM((27, 64, 128), BF),
            pltpu.VMEM((128, 1024), BF),
            pltpu.VMEM((128, 1024), BF),
            pltpu.VMEM((16, 32, LANES), BF),
            pltpu.VMEM((16, 32, LANES), BF),
            pltpu.VMEM((10, 288, 1024), BF),
            pltpu.VMEM((10, 192, 1024), F32),
            pltpu.VMEM((8, 64, 1024), BF),
            pltpu.VMEM((192, 288), BF),
            pltpu.VMEM((1024, 512), BF),
            pltpu.VMEM((16, 32, LANES), BF),
            pltpu.VMEM((16, 32, LANES), BF),
            pltpu.VMEM((384, 576), BF),
            pltpu.VMEM((192, 1152), BF),
            pltpu.VMEM((576, 1024), BF),
            pltpu.VMEM((384, 1024), BF),
            pltpu.VMEM((1152, 1024), BF),
            pltpu.VMEM((576, 384), F32),
            pltpu.VMEM((16, 32, LANES), BF),
            pltpu.VMEM((16, 32, LANES), BF),
            pltpu.VMEM((512, LANES), BF),
            pltpu.VMEM((12, 64, 1024), BF),
            pltpu.VMEM((288, 256), F32),
            dma((9,)), dma((2,)), dma((2,)), dma((15,)), dma((15,)), dma((15,)), dma((15,)),
        ]
        + Sum.scratch(TILES1, ROWS1, F32)
        + Sum.scratch(TILES2, ROWS2, BF),
        compiler_params=pltpu.CompilerParams(
            vmem_limit_bytes=56 << 20, collective_id=0, has_side_effects=True
        ),
    )(
        volumes, jnp.swapaxes(kernel_first, 1, 2), bias_first.reshape(1, -1),
        jnp.swapaxes(kernel_second, 1, 2), bias_second.reshape(1, -1), grad_out,
    )
    feat, out1, out2, outb1, outb2 = pl.pallas_call(
        functools.partial(finish_kernel, scale_one, scale_two),
        name="finish",
        out_shape=[
            shape((1, 128, 1024)), shape((27, 32, 64), F32), shape((27, 64, 128), F32),
            shape((1, 64), F32), shape((1, 128), F32),
        ],
        in_specs=[anywhere] * 3,
        out_specs=[vmem] * 5,
        scratch_shapes=[
            pltpu.VMEM((128, 1024), BF),
            pltpu.VMEM((PARTS, TILES1, ROWS1, LANES), F32),
            pltpu.VMEM((PARTS, TILES2, ROWS2, LANES), BF),
            dma((3,)),
        ],
        compiler_params=pltpu.CompilerParams(vmem_limit_bytes=56 << 20),
    )(feat, sums1, sums2)
    out1, out2 = jnp.swapaxes(out1, 1, 2), jnp.swapaxes(out2, 1, 2)
    return feat, out1, outb1.reshape(-1), out2, outb2.reshape(-1)


def solution(mesh):
    in_specs = (P("sample", None, "space"), P(("sample", "space"), None, None), P(), P(), P(), P())
    out_specs = (P(("sample", "space"), None, None), P(), P(), P(), P())
    return jax.shard_map(
        on_device, mesh=mesh, in_specs=in_specs, out_specs=out_specs, check_vma=False
    )
```
